32 devices in a mesh: row: 4 (over y, x), col: 8 (over z, core).
Axes of the slice: x: 2, y: 2, z: 4, core: 2. Of those that a mesh axis runs over, the one named last changes fastest.
Arguments:
- patterns: bfloat16 [512, 256, 256], P(('row', 'col')), may hold values from -8 to 8, as said below
- ref_spectrum: float32 [2, 256, 256], replicated, may hold values from -6 to 6
- shifts: int32 [512, 2], P(('row', 'col')), may hold values from -16 to 16
- bin_owner: int32 [512, 1], P(('row', 'col')), may hold values from 0 to 7; in each aligned block of 16 rows (0 to 15, 16 to 31, ...) at most 4 rows name the same one
- bin_index: int32 [512], P(('row', 'col')), may hold values from 0 to 3
Outputs:
- final_reference: float32 [2, 256, 256], replicated
- weights: float32 [512], P(('row', 'col'))
- binned: float32 [128, 256, 256], P(('row', 'col'))
The draws below stay inside these ranges and needn't reach their ends.
Inputs may be any that keep to these rules, and one draw needn't show every extreme that they name: `bin_owner`: in the 16 patterns of each block of probe positions, no value is named more than 4 times, a bound that some block reaches. `patterns`: each pattern is displaced by minus its shifts and by a residual shift that is not given.
All inputs are finite; a program needn't handle non-finite values.
Results may differ from the reference program's by a relative error of at most 0.0037.
Values may be sent and summed in bfloat16 or wider, within the bound.
No kernel may reach another device: no remote copies, remote signals or barrier semaphores. Data moves between devices by JAX's collectives and lax.ppermute only.
A program may use at most 128 MiB of HBM per device.

```python
import math
import jax
import jax.numpy as jnp
import numpy as np
from jax import lax

K = 256
PAT_DEV = 16
BINS = 4
ITERS = 2
NPAT = 512
MOST = 4
N_ROW = 4
N_COL = 8


def shift_plan(key):
    base = jax.random.fold_in(key, 7)
    key_nominal, key_member, key_main, key_spread = jax.random.split(base, 4)
    nominal = jax.random.randint(key_nominal, (NPAT, 2), -16, 17, dtype=jnp.int32)
    nominal = nominal.at[0].set(jnp.array([-16, 16], dtype=jnp.int32))
    member = jax.random.randint(key_member, (NPAT, 1), 0, 10, dtype=jnp.int32) < 3
    main_offset = jax.random.randint(key_main, (1, 2), -8, 9, dtype=jnp.int32)
    spread_offset = jax.random.randint(key_spread, (NPAT, 2), -8, 9, dtype=jnp.int32)
    residual = jnp.where(member, main_offset, spread_offset)
    return (nominal, residual)


def draw_shifts(key, part):
    nominal, residual = shift_plan(key)
    return nominal


def draw_patterns(key, part):
    nominal, residual = shift_plan(key)
    base = jax.random.fold_in(key, 11)
    key_common, key_noise, key_gain = jax.random.split(base, 3)
    common = jax.random.truncated_normal(key_common, -4.0, 4.0, (K, K), jnp.float32)
    noise = jax.random.truncated_normal(key_noise, -4.5, 4.5, (NPAT, K, K), jnp.float32)
    log_gain = jax.random.uniform(key_gain, (NPAT,), jnp.float32, math.log(0.8), math.log(2.5))
    strength = jnp.exp(log_gain) / math.sqrt(max(0.3 * NPAT, 16.0))
    displace = residual - nominal
    pixels = jnp.arange(K, dtype=jnp.int32)
    row_index = jnp.mod(pixels[None, :] - displace[:, 0:1], K)
    col_index = jnp.mod(pixels[None, :] - displace[:, 1:2], K)
    moved = common[row_index[:, :, None], col_index[:, None, :]]
    value = strength[:, None, None] * moved + noise
    return value.astype(jnp.bfloat16)


def plant(drawn, own_key, smallest, high):
    place = [jax.random.randint(jax.random.fold_in(own_key, axis), (), 0, length) for axis, length in enumerate(drawn.shape)]
    main_axis = drawn.shape.index(max(drawn.shape))
    next_to = place[:main_axis] + [(place[main_axis] + 1) % drawn.shape[main_axis]] + place[main_axis + 1:]
    return drawn.at[tuple(place)].set(smallest).at[tuple(next_to)].set(high)


def deal_out(rng, own, number, rows, number_of, top, bound, skew):
    ranking = jax.random.permutation(rng, number_of)
    crowded, usual = shares(number_of, rows * top, bound, skew, True), shares(number_of, rows * top, bound, skew, False)
    places = jnp.arange(number_of)

    def named(tallies, offset_by):
        used = int((tallies > 0).sum())
        fixed = max(1, used // 4)
        passed = fixed + (places - fixed + offset_by * (used - fixed)) % max(1, number_of - fixed)
        return jnp.zeros((number_of,), jnp.int32).at[ranking[jnp.where(places < fixed, places, passed)]].set(jnp.asarray(tallies, jnp.int32))

    tallies = jnp.where(number % 4 == 0, named(crowded, number // 4), named(usual, number - number // 4 - 1))
    mixed = jax.random.permutation(jax.random.fold_in(own, 3), number_of)
    source_of, sink = mixed[0:number_of // 2 * 2:2], mixed[1:number_of // 2 * 2:2]
    margin = jnp.minimum(tallies[source_of] - 1, bound - tallies[sink]) // 2
    margin = jnp.where((source_of == ranking[0]) | (sink == ranking[0]) | (tallies[sink] == 0), 0, jnp.maximum(margin, 0))
    passed = jax.random.randint(jax.random.fold_in(own, 4), (number_of // 2,), 0, 1 << 20) % (margin + 1)
    tallies = tallies.at[source_of].add(-passed).at[sink].add(passed)
    members = jnp.searchsorted(jnp.cumsum(tallies), jnp.arange(rows * top), side="right").astype(jnp.int32)
    grid = members.reshape(top, rows).T
    grid = grid[jax.random.permutation(jax.random.fold_in(own, 1), rows)]
    offset_by = jax.random.randint(jax.random.fold_in(own, 2), (rows, 1), 0, top)
    return jnp.take_along_axis(grid, (jnp.arange(top)[None, :] + offset_by) % top, axis=1)


def shares(amount, total, reach, lean, full):
    portions = [(1 << 20) // math.isqrt(standing ** lean) + 1 for standing in range(1, amount + 1)]
    largest = reach if full else min(reach, max(-(-total // amount), total * portions[0] // sum(portions)))
    least = 1 if total - largest >= amount - 1 else 0
    holding, surplus = [largest] + [least] * (amount - 1), total - largest - least * (amount - 1)
    while surplus > 0:
        movable = [i for i in range(1, amount) if holding[i] < largest] or [i for i in range(1, amount) if holding[i] < reach]
        pool, remaining = sum([portions[i] for i in movable]), surplus
        for i in movable:
            addition = min(reach - holding[i], max(1, remaining * portions[i] // pool), surplus)
            holding[i] = holding[i] + addition
            surplus = surplus - addition
    return np.array(holding)


def gaussian(rng, shape, width, reach, held_as=jnp.bfloat16):
    entries = width * jax.random.normal(rng, shape, jnp.float32)
    return jnp.clip(entries, min=-reach, max=reach).astype(held_as)


def setup_inputs(seed: int = 0) -> dict:
    key_of = jax.random.split(jax.random.key(seed), 6)
    patterns = draw_patterns(jax.random.fold_in(key_of[5], 71), 0)
    ref_spectrum = gaussian(key_of[1], (2, K, K), 1.0, 6.0, jnp.float32)
    shifts = draw_shifts(jax.random.fold_in(key_of[5], 71), 0)
    bin_owner_keys = jax.random.split(jax.random.fold_in(key_of[3], 1), NPAT // PAT_DEV)
    bin_owner_turns = jax.random.permutation(jax.random.fold_in(key_of[3], 3), NPAT // PAT_DEV)
    bin_owner = jax.vmap(lambda own, number: deal_out(jax.random.fold_in(key_of[3], 2), own, number, PAT_DEV, N_COL, 1, MOST, 2))(bin_owner_keys, bin_owner_turns).reshape((NPAT, 1))
    bin_index = plant(jax.random.randint(key_of[4], (NPAT,), 0, BINS), jax.random.fold_in(key_of[4], 1), 0, BINS - 1).astype(jnp.int32)
    return dict(patterns=patterns, ref_spectrum=ref_spectrum, shifts=shifts, bin_owner=bin_owner, bin_index=bin_index)


def dft_tables(extent):
    indices = jnp.arange(extent, dtype=jnp.int32)
    product = jnp.mod(indices[:, None] * indices[None, :], extent)
    angles = product.astype(jnp.float32) * (2.0 * math.pi / extent)
    return (jnp.cos(angles).astype(jnp.bfloat16), jnp.sin(angles).astype(jnp.bfloat16))

def stacked_tables(extent):
    cosine, sine = dft_tables(extent)
    fwd_one = jnp.stack([cosine, sine], axis=1)
    fwd_two = jnp.stack([jnp.stack([cosine, -sine]), jnp.stack([-sine, -cosine])])
    inv_one = jnp.stack([jnp.stack([cosine, sine], axis=1), jnp.stack([-sine, cosine], axis=1)])
    inv_two = jnp.stack([cosine, -sine])
    return (fwd_one, fwd_two, inv_one, inv_two)

def forward(pattern_block, fwd_one, fwd_two):
    half_section = jnp.einsum('bij,jtk->bitk', pattern_block.astype(jnp.float32), fwd_one.astype(jnp.float32), precision=lax.Precision.HIGHEST).astype(jnp.bfloat16)
    return jnp.einsum('otij,bjtk->boik', fwd_two.astype(jnp.float32), half_section.astype(jnp.float32), precision=lax.Precision.HIGHEST).astype(jnp.bfloat16)

def phase_ramp(shift_block, extent):
    freqs = jnp.arange(extent, dtype=jnp.int32)
    shift_rows = shift_block[:, 0][:, None, None]
    shift_cols = shift_block[:, 1][:, None, None]
    product = jnp.mod(freqs[None, :, None] * shift_rows + freqs[None, None, :] * shift_cols, extent)
    angles = product.astype(jnp.float32) * (2.0 * math.pi / extent)
    return (jnp.cos(angles), jnp.sin(angles))

def correlate(spec_block, cos_ramp, sin_ramp, ref_now, inv_one, inv_two):
    extent = spec_block.shape[-1]
    spec_re = spec_block[:, 0].astype(jnp.float32)
    spec_im = spec_block[:, 1].astype(jnp.float32)
    aligned_re = spec_re * cos_ramp + spec_im * sin_ramp
    aligned_im = spec_im * cos_ramp - spec_re * sin_ramp
    cross_re = aligned_re * ref_now[0] + aligned_im * ref_now[1]
    cross_im = aligned_im * ref_now[0] - aligned_re * ref_now[1]
    cross = jnp.stack([cross_re, cross_im], axis=1).astype(jnp.bfloat16)
    half_section = jnp.einsum('btik,tkol->biol', cross.astype(jnp.float32), inv_one.astype(jnp.float32), precision=lax.Precision.HIGHEST).astype(jnp.bfloat16)
    corr_map = jnp.einsum('oij,bjol->bil', inv_two.astype(jnp.float32), half_section.astype(jnp.float32), precision=lax.Precision.HIGHEST) / (extent * extent)
    peak_value = lax.optimization_barrier(jnp.max(corr_map, axis=(1, 2)))
    spread = jnp.sqrt(lax.optimization_barrier(jnp.mean(corr_map * corr_map, axis=(1, 2))) + 1e-06)
    weight = peak_value / spread
    local_term = jnp.stack([lax.optimization_barrier(jnp.sum(weight[:, None, None] * aligned_re, axis=0)), lax.optimization_barrier(jnp.sum(weight[:, None, None] * aligned_im, axis=0))])
    return (weight, local_term)

def normalize(summed):
    power = jnp.mean(summed[0] * summed[0] + summed[1] * summed[1])
    return summed / jnp.sqrt(power + 1e-06)

def reference(patterns, ref_spectrum, shifts, bin_owner, bin_index):
    fwd_one, fwd_two, inv_one, inv_two = stacked_tables(K)
    blocks = NPAT // PAT_DEV
    pattern_blocks = patterns.reshape(blocks, PAT_DEV, K, K)
    shift_blocks = shifts.reshape(blocks, PAT_DEV, 2)
    spectra = lax.map(lambda block: forward(block, fwd_one, fwd_two), pattern_blocks)
    ref_now = ref_spectrum
    weight_list = []
    for iteration in range(ITERS):

        def one_block(carry, inputs, ref_now=ref_now):
            spec_block, shift_block = inputs
            cos_ramp, sin_ramp = phase_ramp(shift_block, K)
            weight, local_term = correlate(spec_block, cos_ramp, sin_ramp, ref_now, inv_one, inv_two)
            return (carry + local_term, weight)
        summed, block_weights = lax.scan(one_block, jnp.zeros((2, K, K), jnp.float32), (spectra, shift_blocks))
        ref_now = normalize(summed)
        weight_list.append(block_weights.reshape(-1))
    first_weight = weight_list[0]
    scaled = (first_weight[:, None, None] * patterns.astype(jnp.float32)).astype(jnp.bfloat16)
    scaled = lax.optimization_barrier(scaled).astype(jnp.float32)
    scan_index = jnp.arange(NPAT, dtype=jnp.int32)
    outer = scan_index // PAT_DEV // N_COL
    targets = ((outer * N_COL + bin_owner.reshape(-1)) * BINS + bin_index.reshape(-1)).astype(jnp.int32)
    binned = jax.ops.segment_sum(scaled.reshape(NPAT, K * K), targets, num_segments=N_ROW * N_COL * BINS)
    return (ref_now, weight_list[-1], binned.reshape(N_ROW * N_COL * BINS, K, K))
```

```python
import functools
import math

import jax
import jax.numpy as jnp
import ml_dtypes
import numpy as np
from jax import lax
from jax.experimental import pallas as pl
from jax.experimental.pallas import tpu as pltpu
from jax.sharding import PartitionSpec as P

BINS = 4
ITERS = 2
K = 256
HALF = K // 2
ROWS = HALF + 16
REACH = 16
SLICES = 32
BOTH = ("row", "col")
F32 = jnp.float32
BF16 = jnp.bfloat16


@functools.cache
def tables():
    index = np.arange(K)
    angle = ((index[:, None] * index[None, :]) % K).astype(np.float32) * np.float32(2.0 * math.pi / K)
    cosine = np.cos(angle).astype(ml_dtypes.bfloat16).astype(np.float32)
    sine = np.sin(angle).astype(ml_dtypes.bfloat16).astype(np.float32)
    fwd_one = np.concatenate([cosine, sine], axis=1)
    fwd_two = np.zeros((2 * ROWS, 2 * K), np.float32)
    fwd_two[: HALF + 1, :K] = cosine[: HALF + 1]
    fwd_two[: HALF + 1, K:] = -sine[: HALF + 1]
    fwd_two[ROWS : ROWS + HALF + 1, :K] = -sine[: HALF + 1]
    fwd_two[ROWS : ROWS + HALF + 1, K:] = -cosine[: HALF + 1]
    inv_one = np.block([[cosine, sine], [-sine, cosine]])
    inv_two = np.concatenate([2.0 * cosine[:, :HALF], -2.0 * sine[:, :HALF]], axis=1)
    inv_two[:, 0] = cosine[:, 0]
    inv_two[:, HALF] = cosine[:, HALF]
    flip = np.zeros((K, K), np.float32)
    flip[(K - index) % K, index] = 1.0
    step = np.arange(-REACH, REACH + 1)
    phase = 2.0 * math.pi / K * ((step[:, None] * index[None, :]) % K)
    across = np.zeros((2, 40, K), np.float32)
    across[0, : 2 * REACH + 1] = np.cos(phase)
    across[1, : 2 * REACH + 1] = -np.sin(phase)
    down = np.zeros((2, ROWS, 128), np.float32)
    down[:, :, :40] = across[:, :, :ROWS].transpose(0, 2, 1)
    half = lambda a: a.astype(ml_dtypes.bfloat16)
    return dict(
        fwd_one=half(fwd_one),
        fwd_two=half(fwd_two),
        inv_one=half(inv_one),
        inv_two=half(inv_two),
        flip=half(flip),
        across=across,
        down=down,
    )


def dot(a, b):
    return jnp.dot(a, b, preferred_element_type=F32)


def split(a):
    high = a.astype(BF16)
    return (high, (a - high.astype(F32)).astype(BF16))


def hermitian_part(ref_ref, flip_ref, now_ref):
    flip_rows = flip_ref[:ROWS, :]
    flip_lanes = flip_ref[...]
    for part, sign in ((0, 1.0), (1, -1.0)):
        turned = jnp.zeros((ROWS, K), F32)
        for piece in split(ref_ref[part]):
            turned = turned + dot(dot(flip_rows, piece).astype(BF16), flip_lanes)
        now_ref[part * ROWS : (part + 1) * ROWS, :] = 0.5 * (ref_ref[part, :ROWS, :] + sign * turned)


def unpack(sums_ref, flip_ref):
    slices = sums_ref.shape[0]
    deep = 2 * HALF // slices
    rows = []
    for number in range(slices):
        piece = sums_ref[number].astype(F32)
        rows.append(jnp.concatenate([piece[:deep], piece[deep:]], axis=1))
    whole = jnp.concatenate(rows, axis=0)
    real, imag = whole[:HALF], whole[HALF:]
    first = jnp.concatenate([real[:8], imag[:8]], axis=0)
    turned = dot(first.astype(BF16), flip_ref[...])
    zero_re, zero_im = real[:1], imag[:1]
    turn_re, turn_im = turned[:1], turned[8:9]
    power = (
        2.0 * jnp.sum(whole * whole, axis=(0, 1), keepdims=True)
        - jnp.sum(zero_re * zero_re + zero_im * zero_im, axis=(0, 1), keepdims=True)
    ) * (1.0 / (K * K))
    is_first = lax.broadcasted_iota(jnp.int32, (HALF, K), 0) == 0
    real = jnp.where(is_first, 0.5 * (zero_re + turn_re), real)
    imag = jnp.where(is_first, 0.5 * (zero_im - turn_im), imag)
    last_re = 0.5 * (zero_im + turn_im)
    last_im = 0.5 * (turn_re - zero_re)
    return (real, imag, last_re, last_im, lax.rsqrt(power + 1e-06))


def pack(total_ref, out_ref):
    slices = out_ref.shape[0]
    deep = 2 * HALF // slices
    is_first = lax.broadcasted_iota(jnp.int32, (HALF, K), 0) == 0
    real = total_ref[:HALF, :]
    imag = total_ref[ROWS : ROWS + HALF, :]
    last_re = total_ref[HALF : HALF + 1, :]
    last_im = total_ref[ROWS + HALF : ROWS + HALF + 1, :]
    whole = jnp.concatenate(
        [jnp.where(is_first, real - last_im, real), jnp.where(is_first, imag + last_re, imag)], axis=0
    )
    for number in range(slices):
        piece = whole[number * deep : (number + 1) * deep]
        out_ref[number] = jnp.concatenate([piece[:, :128], piece[:, 128:]], axis=0).astype(BF16)


def correlate(spec, now_ref, inv_one_ref, inv_two_ref):
    spec_re, spec_im = spec[:ROWS].astype(F32), spec[ROWS:].astype(F32)
    now_re, now_im = now_ref[:ROWS, :], now_ref[ROWS:, :]
    cross = jnp.concatenate(
        [spec_re * now_re + spec_im * now_im, spec_im * now_re - spec_re * now_im], axis=1
    ).astype(BF16)
    mid = dot(cross, inv_one_ref[...])
    is_first = lax.broadcasted_iota(jnp.int32, (HALF, K), 0) == 0
    lower = jnp.where(is_first, mid[HALF : HALF + 1, :K], mid[:HALF, K:])
    mid = jnp.concatenate([mid[:HALF, :K], lower], axis=0).astype(BF16)
    corr = dot(inv_two_ref[...], mid)
    peak = jnp.max(corr, axis=(0, 1), keepdims=True) * (1.0 / (K * K))
    mean = jnp.sum(corr * corr, axis=(0, 1), keepdims=True) * (1.0 / float(K) ** 6)
    return peak / jnp.sqrt(mean + 1e-06)


def add_aligned(spec, weight, shift, down_ref, across_ref, total):
    index_y, index_x = shift
    lane = jnp.full((ROWS, 128), index_y, jnp.int32)
    down_re = weight * jnp.take_along_axis(down_ref[0], lane, axis=1, mode="promise_in_bounds")
    down_im = weight * jnp.take_along_axis(down_ref[1], lane, axis=1, mode="promise_in_bounds")
    down_re = jnp.concatenate([down_re, down_re], axis=1)
    down_im = jnp.concatenate([down_im, down_im], axis=1)
    across_re = across_ref[0, pl.ds(index_x, 1), :]
    across_im = across_ref[1, pl.ds(index_x, 1), :]
    ramp_re = down_re * across_re - down_im * across_im
    ramp_im = down_re * across_im + down_im * across_re
    spec_re, spec_im = spec[:ROWS].astype(F32), spec[ROWS:].astype(F32)
    return (
        total[0] + (spec_re * ramp_re - spec_im * ramp_im),
        total[1] + (spec_im * ramp_re + spec_re * ramp_im),
    )


def gather_step(specs, shifts_ref, first, now_ref, inv_one_ref, inv_two_ref, down_ref, across_ref, total_ref, weight_ref):
    total = (total_ref[:ROWS, :], total_ref[ROWS:, :])
    for number, spec in enumerate(specs):
        weight = correlate(spec, now_ref, inv_one_ref, inv_two_ref)
        weight_ref[pl.ds(first + number, 1), :] = jnp.broadcast_to(weight, (1, 128))
        shift = (shifts_ref[first + number, 0] + REACH, shifts_ref[first + number, 1] + REACH)
        total = add_aligned(spec, weight, shift, down_ref, across_ref, total)
    total_ref[:ROWS, :] = total[0]
    total_ref[ROWS:, :] = total[1]


def first_kernel(
    shifts_ref, pattern_ref, ref_ref, fwd_one_ref, fwd_two_ref, inv_one_ref, inv_two_ref, flip_ref, down_ref, across_ref,
    spec_ref, sums_ref, weight_ref, now_ref, total_ref, mid_ref,
):
    step = pl.program_id(0)
    count = pattern_ref.shape[0]

    @pl.when(step == 0)
    def _():
        hermitian_part(ref_ref, flip_ref, now_ref)
        total_ref[...] = jnp.zeros_like(total_ref)

    specs = []
    for number in range(count):
        half = dot(pattern_ref[number], fwd_one_ref[...]).astype(BF16)
        mid_ref[number, :K, :] = half[:, :K]
        mid_ref[number, K:, :] = half[:, K:]
        spec = dot(fwd_two_ref[...], mid_ref[number]).astype(BF16)
        spec_ref[number] = spec
        specs.append(spec)
    gather_step(
        specs, shifts_ref, step * count, now_ref, inv_one_ref, inv_two_ref, down_ref, across_ref, total_ref, weight_ref
    )

    @pl.when(step == pl.num_programs(0) - 1)
    def _():
        pack(total_ref, sums_ref)


def second_kernel(
    shifts_ref, spec_ref, old_ref, inv_one_ref, inv_two_ref, flip_ref, down_ref, across_ref,
    sums_ref, weight_ref, now_ref, total_ref,
):
    step = pl.program_id(0)
    count = spec_ref.shape[0]

    @pl.when(step == 0)
    def _():
        real, imag, last_re, last_im, scale = unpack(old_ref, flip_ref)
        is_first = lax.broadcasted_iota(jnp.int32, (ROWS - HALF, K), 0) == 0
        now_ref[:HALF, :] = real * scale
        now_ref[HALF:ROWS, :] = jnp.where(is_first, last_re * scale, 0.0)
        now_ref[ROWS : ROWS + HALF, :] = imag * scale
        now_ref[ROWS + HALF :, :] = jnp.where(is_first, last_im * scale, 0.0)
        total_ref[...] = jnp.zeros_like(total_ref)

    specs = [spec_ref[number] for number in range(count)]
    gather_step(
        specs, shifts_ref, step * count, now_ref, inv_one_ref, inv_two_ref, down_ref, across_ref, total_ref, weight_ref
    )

    @pl.when(step == pl.num_programs(0) - 1)
    def _():
        pack(total_ref, sums_ref)


def last_kernel(old_ref, flip_ref, out_ref):
    real, imag, last_re, last_im, scale = unpack(old_ref, flip_ref)
    out_ref[0, :HALF, :] = real * scale
    out_ref[1, :HALF, :] = imag * scale
    row = lax.broadcasted_iota(jnp.int32, (HALF, HALF), 0)
    column = lax.broadcasted_iota(jnp.int32, (HALF, HALF), 1)
    turn = jnp.where(row + column == HALF, 1.0, 0.0).astype(BF16)
    is_first = lax.broadcasted_iota(jnp.int32, (HALF, K), 0) == 0
    for part, (body, row_128) in enumerate(((real, last_re), (imag, last_im))):
        turned = dot(dot(turn, body.astype(BF16)).astype(BF16), flip_ref[...])
        turned = turned if part == 0 else -turned
        out_ref[part, HALF:, :] = jnp.where(is_first, row_128, turned) * scale


def add_kernel(in_ref, out_ref):
    total = in_ref[0].astype(F32)
    for number in range(1, in_ref.shape[0]):
        total = total + in_ref[number].astype(F32)
    total = total.astype(BF16)
    for number in range(out_ref.shape[0]):
        out_ref[number] = total


def bin_kernel(target_ref, pattern_ref, weight_ref, mine_ref, other_ref, total_ref):
    bins = mine_ref.shape[0]
    total_ref[...] = jnp.zeros_like(total_ref)
    for number in range(pattern_ref.shape[0]):
        weight = weight_ref[number : number + 1, :]
        weight = jnp.concatenate([weight, weight], axis=1)
        scaled = (weight * pattern_ref[number].astype(F32)).astype(BF16).astype(F32)
        slot = target_ref[number]
        total_ref[pl.ds(slot, 1)] += scaled[None]
    for number in range(bins):
        mine_ref[number] = total_ref[number].astype(BF16)
        other_ref[number] = total_ref[bins + number].astype(BF16)


def whole(array):
    return pl.BlockSpec(array.shape, lambda *_: (0,) * array.ndim)


PARAMS = pltpu.CompilerParams(vmem_limit_bytes=48 * 1024 * 1024)


def run_first(patterns, ref_spectrum, shifts, slices, block):
    t = tables()
    constants = [jnp.asarray(t[name]) for name in ("fwd_one", "fwd_two", "inv_one", "inv_two", "flip", "down", "across")]
    count = patterns.shape[0]
    return pl.pallas_call(
        first_kernel,
        out_shape=(
            jax.ShapeDtypeStruct((count, 2 * ROWS, K), BF16),
            jax.ShapeDtypeStruct((slices, 2 * K * K // 2 // slices // 128, 128), BF16),
            jax.ShapeDtypeStruct((count, 128), F32),
        ),
        grid_spec=pltpu.PrefetchScalarGridSpec(
            num_scalar_prefetch=1,
            grid=(count // block,),
            in_specs=[pl.BlockSpec((block, K, K), lambda i, s: (i, 0, 0)), whole(ref_spectrum)]
            + [whole(c) for c in constants],
            out_specs=(
                pl.BlockSpec((block, 2 * ROWS, K), lambda i, s: (i, 0, 0)),
                pl.BlockSpec((slices, 2 * K * K // 2 // slices // 128, 128), lambda i, s: (0, 0, 0)),
                pl.BlockSpec((count, 128), lambda i, s: (0, 0)),
            ),
            scratch_shapes=[
                pltpu.VMEM((2 * ROWS, K), F32),
                pltpu.VMEM((2 * ROWS, K), F32),
                pltpu.VMEM((block, 2 * K, K), BF16),
            ],
        ),
        compiler_params=PARAMS,
        cost_estimate=pl.CostEstimate(flops=int(5e9), bytes_accessed=int(8e6), transcendentals=0),
        name="forward_and_correlate",
    )(shifts, patterns, ref_spectrum, *constants)


def run_second(spectra, sums, shifts, block):
    t = tables()
    constants = [jnp.asarray(t[name]) for name in ("inv_one", "inv_two", "flip", "down", "across")]
    count = spectra.shape[0]
    return pl.pallas_call(
        second_kernel,
        out_shape=(jax.ShapeDtypeStruct(sums.shape, BF16), jax.ShapeDtypeStruct((count, 128), F32)),
        grid_spec=pltpu.PrefetchScalarGridSpec(
            num_scalar_prefetch=1,
            grid=(count // block,),
            in_specs=[pl.BlockSpec((block, 2 * ROWS, K), lambda i, s: (i, 0, 0)), whole(sums)]
            + [whole(c) for c in constants],
            out_specs=(
                pl.BlockSpec(sums.shape, lambda i, s: (0, 0, 0)),
                pl.BlockSpec((count, 128), lambda i, s: (0, 0)),
            ),
            scratch_shapes=[pltpu.VMEM((2 * ROWS, K), F32), pltpu.VMEM((2 * ROWS, K), F32)],
        ),
        compiler_params=PARAMS,
        cost_estimate=pl.CostEstimate(flops=int(3e9), bytes_accessed=int(4e6), transcendentals=0),
        name="correlate_again",
    )(shifts, spectra, sums, *constants)


def run_last(sums):
    flip = jnp.asarray(tables()["flip"])
    return pl.pallas_call(
        last_kernel, out_shape=jax.ShapeDtypeStruct((2, K, K), F32), compiler_params=PARAMS, name="finish"
    )(sums, flip)


def sum_over_all(sums):
    devices = lax.axis_size("row") * lax.axis_size("col")
    pieces = sums.reshape(devices, sums.size // devices // 128, 128)
    pieces = lax.all_to_all(pieces, BOTH, 0, 0, tiled=True)
    pieces = pl.pallas_call(
        add_kernel, out_shape=jax.ShapeDtypeStruct(pieces.shape, BF16), compiler_params=PARAMS, name="add_pieces"
    )(pieces)
    return lax.all_to_all(pieces, BOTH, 0, 0, tiled=True).reshape(sums.shape)


def run_bins(patterns, weights, targets, bins, deep):
    count = patterns.shape[0]
    part = jax.ShapeDtypeStruct((bins // 2, K, K), BF16)
    return pl.pallas_call(
        bin_kernel,
        out_shape=(part, part),
        grid_spec=pltpu.PrefetchScalarGridSpec(
            num_scalar_prefetch=1,
            grid=(K // deep,),
            in_specs=[
                pl.BlockSpec((count, deep, K), lambda i, s: (0, i, 0)),
                pl.BlockSpec((count, 128), lambda i, s: (0, 0)),
            ],
            out_specs=(
                pl.BlockSpec((bins // 2, deep, K), lambda i, s: (0, i, 0)),
                pl.BlockSpec((bins // 2, deep, K), lambda i, s: (0, i, 0)),
            ),
            scratch_shapes=[pltpu.VMEM((bins, deep, K), F32)],
        ),
        compiler_params=PARAMS,
        cost_estimate=pl.CostEstimate(flops=int(4e6), bytes_accessed=int(8e6), transcendentals=0),
        name="bin_partials",
    )(targets, patterns, weights)


def on_device(patterns, ref_spectrum, shifts, bin_owner, bin_index):
    columns = lax.axis_size("col")
    slices = SLICES
    me = lax.axis_index("col")
    owner = bin_owner.reshape(-1)
    pairs = columns // 2
    targets = ((owner % 2) ^ (me % 2)) * (pairs * BINS) + (owner // 2) * BINS + bin_index

    spectra, sums, first_weight = run_first(patterns, ref_spectrum, shifts, slices, 2)
    total = sum_over_all(sums)
    mine, other = run_bins(patterns, first_weight, targets, columns * BINS, 32)
    other = lax.ppermute(other, "col", [(i, i ^ 1) for i in range(columns)])
    chip = (mine.astype(F32) + other.astype(F32)).astype(BF16)
    groups = [list(range(core, columns, 2)) for core in range(2)]
    arrived = lax.all_to_all(chip, "col", 0, 0, axis_index_groups=groups, tiled=True)
    binned = arrived.reshape(pairs, BINS, K, K).astype(F32).sum(axis=0)

    sums, weight = run_second(spectra, total, shifts, 2)
    total = sum_over_all(sums)
    return (run_last(total), weight[:, 0], binned)


def solution(mesh):
    placed = (P(BOTH, None, None), P(), P(BOTH, None), P(BOTH, None), P(BOTH))
    return jax.shard_map(
        on_device,
        mesh=mesh,
        in_specs=placed,
        out_specs=(P(), P(BOTH), P(BOTH, None, None)),
        check_vma=False,
    )
```

```python
import functools
import math

import jax
import jax.numpy as jnp
import ml_dtypes
import numpy as np
from jax import lax
from jax.experimental import pallas as pl
from jax.experimental.pallas import tpu as pltpu
from jax.sharding import PartitionSpec as P

BINS = 4
ITERS = 2
K = 256
HALF = K // 2
ROWS = HALF + 16
REACH = 16
DEEP = 8
SLICES = HALF // DEEP
BOTH = ("row", "col")
F32 = jnp.float32
BF16 = jnp.bfloat16


@functools.cache
def tables():
    index = np.arange(K)
    angle = ((index[:, None] * index[None, :]) % K).astype(np.float32) * np.float32(2.0 * math.pi / K)
    cosine = np.cos(angle).astype(ml_dtypes.bfloat16).astype(np.float32)
    sine = np.sin(angle).astype(ml_dtypes.bfloat16).astype(np.float32)
    order = np.concatenate([index[:HALF], [HALF], K - index[1:HALF]])
    fwd_one = np.concatenate([cosine[:, : HALF + 1], sine[:, 1:HALF]], axis=1)
    fwd_two = np.zeros((2 * ROWS, K), np.float32)
    fwd_two[: HALF + 1] = cosine[: HALF + 1]
    fwd_two[ROWS : ROWS + HALF + 1] = -sine[: HALF + 1]
    inv_one = np.block([[cosine[order], sine[order]], [-sine[order], cosine[order]]])
    inv_two = np.concatenate([2.0 * cosine[:, :HALF], -2.0 * sine[:, :HALF]], axis=1)
    inv_two[:, 0] = cosine[:, 0]
    inv_two[:, HALF] = cosine[:, HALF]
    reorder = np.zeros((K, K), np.float32)
    reorder[order, index] = 1.0
    turn = np.zeros((ROWS, K), np.float32)
    turn[index[: HALF + 1], (K - index[: HALF + 1]) % K] = 1.0
    step = np.arange(-REACH, REACH + 1)
    phase = 2.0 * math.pi / K * ((step[:, None] * index[None, :]) % K)
    across = np.zeros((2, 40, K), np.float32)
    across[0, : 2 * REACH + 1] = np.cos(phase)[:, order]
    across[1, : 2 * REACH + 1] = -np.sin(phase)[:, order]
    down = np.zeros((2, ROWS, 128), np.float32)
    down[0, : HALF + 1, : 2 * REACH + 1] = np.cos(phase)[:, : HALF + 1].T
    down[1, : HALF + 1, : 2 * REACH + 1] = -np.sin(phase)[:, : HALF + 1].T
    half = lambda a: a.astype(ml_dtypes.bfloat16)
    return dict(
        fwd_one=half(fwd_one),
        fwd_two=half(fwd_two),
        inv_one=half(inv_one),
        inv_two=half(inv_two),
        reorder=half(reorder),
        back=half(reorder.T.copy()),
        turn=half(turn),
        across=across,
        down=down,
    )


def dot(a, b):
    return jnp.dot(a, b, preferred_element_type=F32)


def split(a):
    high = a.astype(BF16)
    return (high, (a - high.astype(F32)).astype(BF16))


def negate_columns(a):
    turned = jnp.concatenate([a[:, HALF:], a[:, :HALF]], axis=1)
    lane = lax.broadcasted_iota(jnp.int32, a.shape, 1)
    return jnp.where((lane == 0) | (lane == HALF), a, turned)


def hermitian_part(ref_ref, reorder_ref, turn_ref, now_ref):
    for part, sign in ((0, 1.0), (1, -1.0)):
        straight = jnp.zeros((ROWS, K), F32)
        turned = jnp.zeros((ROWS, K), F32)
        for piece in split(ref_ref[part]):
            piece = dot(piece, reorder_ref[...]).astype(BF16)
            straight = straight + piece[:ROWS].astype(F32)
            turned = turned + dot(turn_ref[...], piece)
        now_ref[part * ROWS : (part + 1) * ROWS, :] = 0.5 * (straight + sign * negate_columns(turned))


def unpack(core, keep_ref, other_ref):
    halves = []
    for ref in (keep_ref, other_ref):
        rows = []
        for number in range(SLICES):
            piece = ref[number].astype(F32)
            rows.append(jnp.concatenate([piece[:DEEP], piece[DEEP:]], axis=1))
        halves.append(jnp.concatenate(rows, axis=0))
    keep, other = halves
    real, imag = jnp.where(core == 0, keep, other), jnp.where(core == 0, other, keep)
    zero_re, zero_im = real[:1], imag[:1]
    turn_re, turn_im = negate_columns(real[:8])[:1], negate_columns(imag[:8])[:1]
    power = (
        2.0 * jnp.sum(real * real + imag * imag, axis=(0, 1), keepdims=True)
        - jnp.sum(zero_re * zero_re + zero_im * zero_im, axis=(0, 1), keepdims=True)
    ) * (1.0 / (K * K))
    is_first = lax.broadcasted_iota(jnp.int32, (HALF, K), 0) == 0
    real = jnp.where(is_first, 0.5 * (zero_re + turn_re), real)
    imag = jnp.where(is_first, 0.5 * (zero_im - turn_im), imag)
    last_re = 0.5 * (zero_im + turn_im)
    last_im = 0.5 * (turn_re - zero_re)
    return (real, imag, last_re, last_im, lax.rsqrt(power + 1e-06))


def pack(core, total_ref, keep_ref, send_ref):
    is_first = lax.broadcasted_iota(jnp.int32, (HALF, K), 0) == 0
    real = total_ref[:HALF, :]
    imag = total_ref[ROWS : ROWS + HALF, :]
    last_re = total_ref[HALF : HALF + 1, :]
    last_im = total_ref[ROWS + HALF : ROWS + HALF + 1, :]
    real, imag = jnp.where(is_first, real - last_im, real), jnp.where(is_first, imag + last_re, imag)
    for ref, half in ((keep_ref, jnp.where(core == 0, real, imag)), (send_ref, jnp.where(core == 0, imag, real))):
        for number in range(SLICES):
            piece = half[number * DEEP : (number + 1) * DEEP]
            ref[number] = jnp.concatenate([piece[:, :128], piece[:, 128:]], axis=0).astype(ref.dtype)


def forward(first, size, pattern_ref, spec_ref, fwd_one_ref, fwd_two_ref):
    flat = pattern_ref[pl.ds(first, size)].reshape(size * K, K)
    half = dot(flat, fwd_one_ref[...]).astype(BF16)
    is_zero = lax.broadcasted_iota(jnp.int32, (ROWS, HALF), 1) == 0
    for number in range(size):
        both = dot(fwd_two_ref[...], half[number * K : (number + 1) * K])
        cu, cv = both[:ROWS, :HALF], both[:ROWS, HALF:]
        su, sv = both[ROWS:, :HALF], both[ROWS:, HALF:]
        real = jnp.concatenate([cu + jnp.where(is_zero, 0.0, sv), jnp.where(is_zero, cv, cu - sv)], axis=1)
        imag = jnp.concatenate([su - jnp.where(is_zero, 0.0, cv), jnp.where(is_zero, sv, su + cv)], axis=1)
        spec_ref[first + number] = jnp.concatenate([real, imag], axis=0).astype(BF16)


def correlate(first, size, spec_ref, now_ref, cross_ref, inv_one_ref, inv_two_ref, weight_ref):
    for number in range(size):
        spec_re = spec_ref[first + number, :ROWS, :].astype(F32)
        spec_im = spec_ref[first + number, ROWS:, :].astype(F32)
        now_re, now_im = now_ref[:ROWS, :], now_ref[ROWS:, :]
        rows = slice(number * ROWS, (number + 1) * ROWS)
        cross_ref[rows, :K] = (spec_re * now_re + spec_im * now_im).astype(BF16)
        cross_ref[rows, K:] = (spec_im * now_re - spec_re * now_im).astype(BF16)
    both = dot(cross_ref[...], inv_one_ref[...])
    is_first = lax.broadcasted_iota(jnp.int32, (HALF, K), 0) == 0
    for number in range(size):
        mid = both[number * ROWS : (number + 1) * ROWS]
        lower = jnp.where(is_first, mid[HALF : HALF + 1, :K], mid[:HALF, K:])
        corr = dot(inv_two_ref[...], jnp.concatenate([mid[:HALF, :K], lower], axis=0).astype(BF16))
        peak = jnp.max(corr, axis=(0, 1), keepdims=True) * (1.0 / (K * K))
        mean = jnp.sum(corr * corr, axis=(0, 1), keepdims=True) * (1.0 / float(K) ** 6)
        weight = peak / jnp.sqrt(mean + 1e-06)
        weight_ref[pl.ds(first + number, 1), :] = jnp.broadcast_to(weight, (1, 128))


def add_aligned(first, size, scalars_ref, spec_ref, weight_ref, down_ref, across_ref, total_ref):
    total_re, total_im = total_ref[:ROWS, :], total_ref[ROWS:, :]
    for number in range(size):
        weight = weight_ref[pl.ds(first + number, 1), :]
        lane = jnp.full((ROWS, 128), scalars_ref[2 * (first + number)] + REACH, jnp.int32)
        down_re = jnp.take_along_axis(down_ref[0], lane, axis=1, mode="promise_in_bounds")
        down_im = jnp.take_along_axis(down_ref[1], lane, axis=1, mode="promise_in_bounds")
        down_re = jnp.concatenate([down_re, down_re], axis=1)
        down_im = jnp.concatenate([down_im, down_im], axis=1)
        weight = jnp.concatenate([weight, weight], axis=1)
        column = scalars_ref[2 * (first + number) + 1] + REACH
        across_re = weight * across_ref[0, pl.ds(column, 1), :]
        across_im = weight * across_ref[1, pl.ds(column, 1), :]
        ramp_re = down_re * across_re - down_im * across_im
        ramp_im = down_re * across_im + down_im * across_re
        spec_re = spec_ref[first + number, :ROWS, :].astype(F32)
        spec_im = spec_ref[first + number, ROWS:, :].astype(F32)
        total_re = total_re + (spec_re * ramp_re - spec_im * ramp_im)
        total_im = total_im + (spec_im * ramp_re + spec_re * ramp_im)
    total_ref[:ROWS, :] = total_re
    total_ref[ROWS:, :] = total_im


def add_bins(first, size, scalars_ref, pattern_ref, weight_ref, bins_ref):
    for number in range(size):
        weight = weight_ref[pl.ds(first + number, 1), :]
        weight = jnp.concatenate([weight, weight], axis=1)
        scaled = (weight * pattern_ref[first + number].astype(F32)).astype(BF16)
        slot = scalars_ref[TARGET + first + number]
        bins_ref[slot] = bins_ref[slot] + scaled


def copies(sources, targets, sems):
    return [pltpu.make_async_copy(a, b, sems.at[i]) for i, (a, b) in enumerate(zip(sources, targets))]


GROUP = 4
COUNT = 16
TARGET = 2 * COUNT
CORE = 3 * COUNT


def first_kernel(
    scalars_ref, pattern_hbm, *refs,
):
    constants, refs = refs[:9], refs[9:]
    spec_hbm, keep_ref, send_ref, weight_ref = refs[:4]
    binned_hbm, refs = refs[4:7], refs[7:]
    held, refs = refs[:9], refs[9:]
    pattern_ref, spec_ref, now_ref, total_ref, cross_ref, bins_ref, const_sem, pattern_sem, spec_sem, bins_sem = refs
    ref_ref, reorder_ref, turn_ref, fwd_one_ref, fwd_two_ref, inv_one_ref, inv_two_ref, down_ref, across_ref = held
    count = pattern_ref.shape[0]
    groups = count // GROUP

    def group(ref, number):
        return ref.at[pl.ds(number * GROUP, GROUP)]

    def fetch(number):
        return pltpu.make_async_copy(group(pattern_hbm, number), group(pattern_ref, number), pattern_sem.at[number])

    def store(number):
        return pltpu.make_async_copy(group(spec_ref, number), group(spec_hbm, number), spec_sem.at[number])

    incoming = copies(constants, held, const_sem)
    for copy in incoming[:3]:
        copy.start()
    fetch(0).start()
    for copy in incoming[3:]:
        copy.start()
    for number in range(1, groups):
        fetch(number).start()
    total_ref[...] = jnp.zeros_like(total_ref)
    weight_ref[...] = jnp.zeros_like(weight_ref)
    bins_ref[...] = jnp.zeros_like(bins_ref)
    spec_ref[:GROUP] = jnp.zeros_like(spec_ref[:GROUP])
    for copy in incoming[:3]:
        copy.wait()
    hermitian_part(ref_ref, reorder_ref, turn_ref, now_ref)
    for copy in incoming[3:]:
        copy.wait()

    def finish(first):
        add_aligned(first, GROUP, scalars_ref, spec_ref, weight_ref, down_ref, across_ref, total_ref)

    def body(number, _):
        first = number * GROUP
        fetch(number).wait()
        last = jnp.maximum(first - GROUP, 0)
        finish(last)
        forward(first, GROUP, pattern_ref, spec_ref, fwd_one_ref, fwd_two_ref)
        store(number).start()
        correlate(first, GROUP, spec_ref, now_ref, cross_ref, inv_one_ref, inv_two_ref, weight_ref)
        add_bins(first, GROUP, scalars_ref, pattern_ref, weight_ref, bins_ref)
        return 0

    lax.fori_loop(0, groups, body, 0)
    place, sources = 0, []
    for target in binned_hbm:
        sources.append(bins_ref.at[pl.ds(place, target.shape[0])])
        place += target.shape[0]
    outgoing = copies(sources, binned_hbm, bins_sem)
    for copy in outgoing:
        copy.start()
    finish(count - GROUP)
    pack(scalars_ref[CORE], total_ref, keep_ref, send_ref)
    for copy in outgoing:
        copy.wait()
    for number in range(groups):
        store(number).wait()


def second_kernel(
    scalars_ref, spec_hbm, old_ref, old_other_ref, *refs,
):
    constants, refs = refs[:4], refs[4:]
    keep_ref, send_ref, weight_ref = refs[:3]
    held, refs = refs[3:7], refs[7:]
    spec_ref, now_ref, total_ref, cross_ref, const_sem, spec_sem = refs
    inv_one_ref, inv_two_ref, down_ref, across_ref = held
    count = spec_ref.shape[0]
    groups = count // GROUP

    def group(ref, number):
        return ref.at[pl.ds(number * GROUP, GROUP)]

    def fetch(number):
        return pltpu.make_async_copy(group(spec_hbm, number), group(spec_ref, number), spec_sem.at[number])

    incoming = copies(constants, held, const_sem)
    fetch(0).start()
    for copy in incoming:
        copy.start()
    for number in range(1, groups):
        fetch(number).start()
    total_ref[...] = jnp.zeros_like(total_ref)
    weight_ref[...] = jnp.zeros_like(weight_ref)
    real, imag, last_re, last_im, scale = unpack(scalars_ref[CORE], old_ref, old_other_ref)
    is_first = lax.broadcasted_iota(jnp.int32, (ROWS - HALF, K), 0) == 0
    now_ref[:HALF, :] = real * scale
    now_ref[HALF:ROWS, :] = jnp.where(is_first, last_re * scale, 0.0)
    now_ref[ROWS : ROWS + HALF, :] = imag * scale
    now_ref[ROWS + HALF :, :] = jnp.where(is_first, last_im * scale, 0.0)
    for copy in incoming:
        copy.wait()

    def finish(first):
        add_aligned(first, GROUP, scalars_ref, spec_ref, weight_ref, down_ref, across_ref, total_ref)

    def body(number, _):
        first = number * GROUP
        fetch(number).wait()
        finish(jnp.maximum(first - GROUP, 0))
        correlate(first, GROUP, spec_ref, now_ref, cross_ref, inv_one_ref, inv_two_ref, weight_ref)
        return 0

    lax.fori_loop(0, groups, body, 0)
    finish(count - GROUP)
    pack(scalars_ref[CORE], total_ref, keep_ref, send_ref)


def last_kernel(scalars_ref, old_ref, old_other_ref, back_ref, out_ref):
    real, imag, last_re, last_im, scale = unpack(scalars_ref[CORE], old_ref, old_other_ref)
    row = lax.broadcasted_iota(jnp.int32, (HALF, HALF), 0)
    column = lax.broadcasted_iota(jnp.int32, (HALF, HALF), 1)
    turn = jnp.where(row + column == HALF, 1.0, 0.0).astype(BF16)
    is_first = lax.broadcasted_iota(jnp.int32, (HALF, K), 0) == 0
    for part, (body, row_128) in enumerate(((real, last_re), (imag, last_im))):
        turned = negate_columns(dot(turn, body.astype(BF16)))
        turned = jnp.where(is_first, row_128, turned if part == 0 else -turned)
        both = jnp.concatenate([body, turned], axis=0)
        natural = sum(dot(piece, back_ref[...]) for piece in split(both))
        out_ref[part] = natural * scale


ANY = pl.BlockSpec(memory_space=pl.ANY)
PARAMS = pltpu.CompilerParams(vmem_limit_bytes=56 * 1024 * 1024)


HALF_SPEC = pl.BlockSpec((SLICES, 2 * DEEP, 128), lambda *_: (0, 0, 0))


def half_sum(dtype):
    return jax.ShapeDtypeStruct((SLICES, 2 * DEEP, 128), dtype)


def constant(*names):
    return [jnp.asarray(tables()[name]) for name in names]


def held_like(arrays):
    return [pltpu.VMEM(a.shape, a.dtype) for a in arrays]


def run_first(patterns, ref_spectrum, scalars, bins):
    arrays = [ref_spectrum] + constant(
        "reorder", "turn", "fwd_one", "fwd_two", "inv_one", "inv_two", "down", "across"
    )
    count = patterns.shape[0]
    spectra = jax.ShapeDtypeStruct((count, 2 * ROWS, K), BF16)
    part = lambda size: jax.ShapeDtypeStruct((size, K, K), BF16)
    parts = (part(bins // 2), part(bins // 2 - BINS), part(BINS))
    return pl.pallas_call(
        first_kernel,
        out_shape=(spectra, half_sum(F32), half_sum(BF16), jax.ShapeDtypeStruct((count, 128), F32), *parts),
        grid_spec=pltpu.PrefetchScalarGridSpec(
            num_scalar_prefetch=1,
            grid=(1,),
            in_specs=[ANY] * (1 + len(arrays)),
            out_specs=(
                ANY,
                HALF_SPEC,
                HALF_SPEC,
                pl.BlockSpec((count, 128), lambda i, *_: (0, 0)),
                ANY,
                ANY,
                ANY,
            ),
            scratch_shapes=held_like(arrays)
            + [
                pltpu.VMEM(patterns.shape, BF16),
                pltpu.VMEM(spectra.shape, BF16),
                pltpu.VMEM((2 * ROWS, K), F32),
                pltpu.VMEM((2 * ROWS, K), F32),
                pltpu.VMEM((GROUP * ROWS, 2 * K), BF16),
                pltpu.VMEM((bins, K, K), BF16),
                pltpu.SemaphoreType.DMA((len(arrays),)),
                pltpu.SemaphoreType.DMA((count // GROUP,)),
                pltpu.SemaphoreType.DMA((count // GROUP,)),
                pltpu.SemaphoreType.DMA((3,)),
            ],
        ),
        compiler_params=PARAMS,
        cost_estimate=pl.CostEstimate(flops=int(5e9), bytes_accessed=int(12e6), transcendentals=0),
        name="forward_and_correlate",
    )(scalars, patterns, *arrays)


def run_second(spectra, keep, other, scalars):
    arrays = constant("inv_one", "inv_two", "down", "across")
    count = spectra.shape[0]
    return pl.pallas_call(
        second_kernel,
        out_shape=(half_sum(F32), half_sum(BF16), jax.ShapeDtypeStruct((count, 128), F32)),
        grid_spec=pltpu.PrefetchScalarGridSpec(
            num_scalar_prefetch=1,
            grid=(1,),
            in_specs=[ANY, HALF_SPEC, HALF_SPEC] + [ANY] * len(arrays),
            out_specs=(HALF_SPEC, HALF_SPEC, pl.BlockSpec((count, 128), lambda i, s: (0, 0))),
            scratch_shapes=held_like(arrays)
            + [
                pltpu.VMEM(spectra.shape, BF16),
                pltpu.VMEM((2 * ROWS, K), F32),
                pltpu.VMEM((2 * ROWS, K), F32),
                pltpu.VMEM((GROUP * ROWS, 2 * K), BF16),
                pltpu.SemaphoreType.DMA((len(arrays),)),
                pltpu.SemaphoreType.DMA((count // GROUP,)),
            ],
        ),
        compiler_params=PARAMS,
        cost_estimate=pl.CostEstimate(flops=int(3e9), bytes_accessed=int(4e6), transcendentals=0),
        name="correlate_again",
    )(scalars, spectra, keep, other, *arrays)


def run_last(keep, other, scalars):
    whole = lambda shape: pl.BlockSpec(shape, lambda *_: (0,) * len(shape))
    return pl.pallas_call(
        last_kernel,
        out_shape=jax.ShapeDtypeStruct((2, K, K), F32),
        grid_spec=pltpu.PrefetchScalarGridSpec(
            num_scalar_prefetch=1,
            grid=(1,),
            in_specs=[HALF_SPEC, HALF_SPEC, whole((K, K))],
            out_specs=whole((2, K, K)),
        ),
        compiler_params=PARAMS,
        cost_estimate=pl.CostEstimate(flops=int(1e8), bytes_accessed=int(1e6), transcendentals=0),
        name="finish",
    )(scalars, keep, other, *constant("back"))


def add_halves(*halves):
    values = [half.astype(F32) for half in halves]
    while len(values) > 1:
        values = [values[i] + values[i + 1] for i in range(0, len(values), 2)]
    return values[0].astype(BF16)


def on_device(patterns, ref_spectrum, shifts, bin_owner, bin_index):
    columns, lines = lax.axis_size("col"), lax.axis_size("row")
    me = lax.axis_index("col")
    owner = bin_owner.reshape(-1)
    chips = columns // 2
    targets = ((owner ^ me) % 2) * (chips * BINS) + ((owner // 2) ^ (me // 2)) * BINS + bin_index
    scalars = jnp.concatenate([shifts.reshape(-1), targets, (me % 2).reshape(1).astype(jnp.int32)])

    def send(array, far, axis="col"):
        return lax.ppermute(array, axis, [(i, i ^ far) for i in range(lax.axis_size(axis))])

    def over_chips(half):
        return [half] + [send(half, 2 * far) for far in range(1, chips)]

    def over_lines(half):
        return [half] + [send(half, far, "row") for far in range(1, lines)]

    spectra, keep, away, _, mine, other, other_far = run_first(patterns, ref_spectrum, scalars, columns * BINS)
    half = add_halves(keep, send(away, 1))
    half, other, other_far = lax.optimization_barrier((half, other, other_far))
    half = add_halves(*over_chips(half))
    other, other_far = send(other, 1), send(other_far, 1)
    mine = mine.reshape(chips, BINS, K, K)
    other = other.reshape(chips - 1, BINS, K, K)

    def chip_bins(far, *more, low=0, high=BINS):
        there = other[far] if far < chips - 1 else other_far
        arrays = [array[low:high].astype(F32) for array in (mine[far], there, *more)]
        return sum(arrays[1:], arrays[0])

    binned = chip_bins(0)
    if chips == 4:
        block = chip_bins(3).astype(BF16)
        half, block = lax.optimization_barrier((half, block))
        pairs = lambda hops: [(2 * a + core, 2 * b + core) for a, b in hops for core in range(2)]
        passing = lax.ppermute(block, "col", pairs([(0, 1), (3, 2)]))
        middle = lax.ppermute(block, "col", pairs([(1, 2), (2, 1)]))
        half = add_halves(*over_lines(half))
        other_half = send(half, 1)
        half, passing, middle = lax.optimization_barrier((half, passing, middle))
        cut = BINS - 1
        blocks = [
            (chip_bins(1, low=low, high=high).astype(BF16), chip_bins(2, passing, low=low, high=high).astype(BF16))
            for low, high in ((0, cut), (cut, BINS))
        ]
        half, other_half, blocks = lax.optimization_barrier((half, other_half, blocks))
        lower = (send(blocks[0][0], 2), send(blocks[0][1], 4))
        keep, away, weight = run_second(spectra, half, other_half, scalars)
        away, lower = lax.optimization_barrier((away, lower))
        half = add_halves(*over_lines(add_halves(keep, send(away, 1))))
        upper = (send(blocks[1][0], 2), send(blocks[1][1], 4))
        half, lower, upper = lax.optimization_barrier((half, lower, upper))
        binned = binned + middle.astype(F32)
        for a, b in zip(lower, upper):
            binned = binned + jnp.concatenate([a, b]).astype(F32)
    else:
        half = add_halves(*over_lines(half))
        for far in range(1, chips):
            binned = binned + send(chip_bins(far).astype(BF16), 2 * far).astype(F32)
        keep, away, weight = run_second(spectra, half, send(half, 1), scalars)
        half = add_halves(*over_lines(add_halves(keep, send(away, 1))))
    half = add_halves(*over_chips(half))
    return (run_last(half, send(half, 1), scalars), weight[:, 0], binned)


def solution(mesh):
    placed = (P(BOTH, None, None), P(), P(BOTH, None), P(BOTH, None), P(BOTH))
    return jax.shard_map(
        on_device,
        mesh=mesh,
        in_specs=placed,
        out_specs=(P(), P(BOTH), P(BOTH, None, None)),
        check_vma=False,
    )
```

```python
import functools
import math

import jax
import jax.numpy as jnp
import ml_dtypes
import numpy as np
from jax import lax
from jax.experimental import pallas as pl
from jax.experimental.pallas import tpu as pltpu
from jax.sharding import PartitionSpec as P

BINS = 4
ITERS = 2
K = 256
HALF = K // 2
ROWS = HALF + 16
REACH = 16
DEEP = 8
SLICES = HALF // DEEP
BOTH = ("row", "col")
F32 = jnp.float32
BF16 = jnp.bfloat16


@functools.cache
def cosine_row():
    angle = np.arange(HALF).astype(np.float32) * np.float32(2.0 * math.pi / K)
    return np.broadcast_to(np.cos(angle).astype(np.float32), (8, HALF))


def iota(shape, axis):
    return lax.broadcasted_iota(jnp.int32, shape, axis)


def cosine(row_ref, turns):
    rows, lanes = turns.shape
    row = jnp.broadcast_to(row_ref[:1, :], (rows, HALF))
    found = []
    for first in range(0, lanes, HALF):
        part = turns[:, first : first + HALF]
        value = jnp.take_along_axis(row, part & (HALF - 1), axis=1, mode="promise_in_bounds")
        found.append(jnp.where((part & HALF) == 0, value, -value))
    return found[0] if len(found) == 1 else jnp.concatenate(found, axis=1)


QUARTER = K // 4


def column_order(index):
    return jnp.where(index <= HALF, index, HALF - index)


def fill_forward(row_ref, fwd_one_ref, fwd_two_ref):
    lane = iota((K, K), 1)
    turns = iota((K, K), 0) * jnp.where(lane <= HALF, lane, lane - HALF)
    fwd_one_ref[...] = cosine(row_ref, turns - jnp.where(lane <= HALF, 0, QUARTER)).astype(BF16)
    row = iota((ROWS, K), 0)
    turns = row * iota((ROWS, K), 1)
    for part in range(2):
        table = jnp.where(row <= HALF, cosine(row_ref, turns + part * QUARTER), 0.0)
        fwd_two_ref[part * ROWS : (part + 1) * ROWS, :] = table.astype(BF16)


def fill_inverse(row_ref, inv_one_ref, inv_two_ref):
    row, lane = iota((K, K), 0), iota((K, K), 1)
    turns = column_order(row) * lane
    even, odd = cosine(row_ref, turns).astype(BF16), cosine(row_ref, turns - QUARTER).astype(BF16)
    inv_one_ref[:K, :K] = even
    inv_one_ref[:K, K:] = odd
    inv_one_ref[K:, :K] = -odd
    inv_one_ref[K:, K:] = even
    turns = row * jnp.where(lane <= HALF, lane, lane - HALF) + jnp.where(lane <= HALF, 0, QUARTER)
    scale = jnp.where((lane == 0) | (lane == HALF), 1.0, 2.0)
    inv_two_ref[...] = (scale * cosine(row_ref, turns).astype(BF16).astype(F32)).astype(BF16)


def one_at(rows, lanes):
    return jnp.where(rows == lanes, 1.0, 0.0).astype(BF16)


def dot(a, b):
    return jnp.dot(a, b, preferred_element_type=F32)


def split(a):
    high = a.astype(BF16)
    return (high, (a - high.astype(F32)).astype(BF16))


def negate_columns(a):
    turned = jnp.concatenate([a[:, HALF:], a[:, :HALF]], axis=1)
    lane = lax.broadcasted_iota(jnp.int32, a.shape, 1)
    return jnp.where((lane == 0) | (lane == HALF), a, turned)


def hermitian_part(ref_ref, now_ref):
    reorder = one_at(iota((K, K), 0), column_order(iota((K, K), 1)) & (K - 1))
    row = iota((ROWS, K), 0)
    turn = one_at(jnp.where(row <= HALF, (K - row) & (K - 1), -1), iota((ROWS, K), 1))
    for part, sign in ((0, 1.0), (1, -1.0)):
        straight = jnp.zeros((ROWS, K), F32)
        turned = jnp.zeros((ROWS, K), F32)
        for piece in split(ref_ref[part]):
            piece = dot(piece, reorder).astype(BF16)
            straight = straight + piece[:ROWS].astype(F32)
            turned = turned + dot(turn, piece)
        now_ref[part * ROWS : (part + 1) * ROWS, :] = 0.5 * (straight + sign * negate_columns(turned))


def unpack(core, keep_ref, other_ref):
    halves = []
    for ref in (keep_ref, other_ref):
        rows = []
        for number in range(SLICES):
            piece = ref[number].astype(F32)
            rows.append(jnp.concatenate([piece[:DEEP], piece[DEEP:]], axis=1))
        halves.append(jnp.concatenate(rows, axis=0))
    keep, other = halves
    real, imag = jnp.where(core == 0, keep, other), jnp.where(core == 0, other, keep)
    zero_re, zero_im = real[:1], imag[:1]
    turn_re, turn_im = negate_columns(real[:8])[:1], negate_columns(imag[:8])[:1]
    power = (
        2.0 * jnp.sum(real * real + imag * imag, axis=(0, 1), keepdims=True)
        - jnp.sum(zero_re * zero_re + zero_im * zero_im, axis=(0, 1), keepdims=True)
    ) * (1.0 / (K * K))
    is_first = lax.broadcasted_iota(jnp.int32, (HALF, K), 0) == 0
    real = jnp.where(is_first, 0.5 * (zero_re + turn_re), real)
    imag = jnp.where(is_first, 0.5 * (zero_im - turn_im), imag)
    last_re = 0.5 * (zero_im + turn_im)
    last_im = 0.5 * (turn_re - zero_re)
    return (real, imag, last_re, last_im, lax.rsqrt(power + 1e-06))


def pack(core, total_ref, keep_ref, send_ref):
    is_first = lax.broadcasted_iota(jnp.int32, (HALF, K), 0) == 0
    real = total_ref[:HALF, :]
    imag = total_ref[ROWS : ROWS + HALF, :]
    last_re = total_ref[HALF : HALF + 1, :]
    last_im = total_ref[ROWS + HALF : ROWS + HALF + 1, :]
    real, imag = jnp.where(is_first, real - last_im, real), jnp.where(is_first, imag + last_re, imag)
    for ref, half in ((keep_ref, jnp.where(core == 0, real, imag)), (send_ref, jnp.where(core == 0, imag, real))):
        for number in range(SLICES):
            piece = half[number * DEEP : (number + 1) * DEEP]
            ref[number] = jnp.concatenate([piece[:, :128], piece[:, 128:]], axis=0).astype(ref.dtype)


def forward(first, size, pattern_ref, spec_ref, fwd_one_ref, fwd_two_ref):
    flat = pattern_ref[pl.ds(first, size)].reshape(size * K, K)
    half = dot(flat, fwd_one_ref[...]).astype(BF16)
    is_zero = lax.broadcasted_iota(jnp.int32, (ROWS, HALF), 1) == 0
    for number in range(size):
        both = dot(fwd_two_ref[...], half[number * K : (number + 1) * K])
        cu, cv = both[:ROWS, :HALF], both[:ROWS, HALF:]
        su, sv = both[ROWS:, :HALF], both[ROWS:, HALF:]
        real = jnp.concatenate([cu + jnp.where(is_zero, 0.0, sv), jnp.where(is_zero, cv, cu - sv)], axis=1)
        imag = jnp.concatenate([su - jnp.where(is_zero, 0.0, cv), jnp.where(is_zero, sv, su + cv)], axis=1)
        spec_ref[first + number] = jnp.concatenate([real, imag], axis=0).astype(BF16)


def correlate(first, size, spec_ref, now_ref, cross_ref, inv_one_ref, inv_two_ref, weight_ref):
    for number in range(size):
        spec_re = spec_ref[first + number, :ROWS, :].astype(F32)
        spec_im = spec_ref[first + number, ROWS:, :].astype(F32)
        now_re, now_im = now_ref[:ROWS, :], now_ref[ROWS:, :]
        rows = slice(number * ROWS, (number + 1) * ROWS)
        cross_ref[rows, :K] = (spec_re * now_re + spec_im * now_im).astype(BF16)
        cross_ref[rows, K:] = (spec_im * now_re - spec_re * now_im).astype(BF16)
    both = dot(cross_ref[...], inv_one_ref[...])
    is_first = lax.broadcasted_iota(jnp.int32, (HALF, K), 0) == 0
    for number in range(size):
        mid = both[number * ROWS : (number + 1) * ROWS]
        lower = jnp.where(is_first, mid[HALF : HALF + 1, :K], mid[:HALF, K:])
        corr = dot(inv_two_ref[...], jnp.concatenate([mid[:HALF, :K], lower], axis=0).astype(BF16))
        peak = jnp.max(corr, axis=(0, 1), keepdims=True) * (1.0 / (K * K))
        mean = jnp.sum(corr * corr, axis=(0, 1), keepdims=True) * (1.0 / float(K) ** 6)
        weight = peak / jnp.sqrt(mean + 1e-06)
        weight_ref[pl.ds(first + number, 1), :] = jnp.broadcast_to(weight, (1, 128))


def add_aligned(first, size, scalars_ref, spec_ref, weight_ref, row_ref, total_ref):
    total_re, total_im = total_ref[:ROWS, :], total_ref[ROWS:, :]
    lane = iota((8, K), 1)
    for number in range(size):
        shift_y, shift_x = scalars_ref[2 * (first + number)], scalars_ref[2 * (first + number) + 1]
        weight = weight_ref[pl.ds(first + number, 1), :]
        weight = jnp.concatenate([weight, weight], axis=1)
        turns = column_order(lane) * shift_x
        across_re = weight * cosine(row_ref, turns)[:1]
        across_im = weight * cosine(row_ref, turns + QUARTER)[:1]
        turns = iota((ROWS, HALF), 0) * shift_y
        down_re, down_im = cosine(row_ref, turns), cosine(row_ref, turns + QUARTER)
        down_re = jnp.concatenate([down_re, down_re], axis=1)
        down_im = jnp.concatenate([down_im, down_im], axis=1)
        ramp_re = down_re * across_re - down_im * across_im
        ramp_im = down_re * across_im + down_im * across_re
        spec_re = spec_ref[first + number, :ROWS, :].astype(F32)
        spec_im = spec_ref[first + number, ROWS:, :].astype(F32)
        total_re = total_re + (spec_re * ramp_re - spec_im * ramp_im)
        total_im = total_im + (spec_im * ramp_re + spec_re * ramp_im)
    total_ref[:ROWS, :] = total_re
    total_ref[ROWS:, :] = total_im


def add_bins(first, size, scalars_ref, pattern_ref, weight_ref, bins_ref):
    for number in range(size):
        weight = weight_ref[pl.ds(first + number, 1), :]
        weight = jnp.concatenate([weight, weight], axis=1)
        scaled = (weight * pattern_ref[first + number].astype(F32)).astype(BF16)
        slot = scalars_ref[TARGET + first + number]
        bins_ref[slot] = bins_ref[slot] + scaled


GROUP = 4
COUNT = 16
TARGET = 2 * COUNT
CORE = 3 * COUNT


def first_kernel(
    scalars_ref, row_ref, pattern_hbm, ref_hbm, spec_ref, keep_ref, send_ref, bins_ref,
    pattern_ref, ref_ref, fwd_one_ref, fwd_two_ref, inv_one_ref, inv_two_ref, now_ref, total_ref, cross_ref,
    weight_ref, ref_sem, pattern_sem,
):
    count = pattern_ref.shape[0]
    groups = count // GROUP

    def fetch(number):
        source, target = (ref.at[pl.ds(number * GROUP, GROUP)] for ref in (pattern_hbm, pattern_ref))
        return pltpu.make_async_copy(source, target, pattern_sem.at[number])

    ref_copy = pltpu.make_async_copy(ref_hbm, ref_ref, ref_sem)
    ref_copy.start()
    for number in range(groups):
        fetch(number).start()
    fill_forward(row_ref, fwd_one_ref, fwd_two_ref)
    fill_inverse(row_ref, inv_one_ref, inv_two_ref)
    total_ref[...] = jnp.zeros_like(total_ref)
    bins_ref[...] = jnp.zeros_like(bins_ref)
    weight_ref[...] = jnp.zeros_like(weight_ref)
    spec_ref[:GROUP] = jnp.zeros_like(spec_ref[:GROUP])
    ref_copy.wait()
    hermitian_part(ref_ref, now_ref)

    def finish(first):
        add_aligned(first, GROUP, scalars_ref, spec_ref, weight_ref, row_ref, total_ref)

    def body(number, _):
        first = number * GROUP
        fetch(number).wait()
        finish(jnp.maximum(first - GROUP, 0))
        forward(first, GROUP, pattern_ref, spec_ref, fwd_one_ref, fwd_two_ref)
        correlate(first, GROUP, spec_ref, now_ref, cross_ref, inv_one_ref, inv_two_ref, weight_ref)
        add_bins(first, GROUP, scalars_ref, pattern_ref, weight_ref, bins_ref)
        return 0

    lax.fori_loop(0, groups, body, 0)
    finish(count - GROUP)
    pack(scalars_ref[CORE], total_ref, keep_ref, send_ref)


def second_kernel(
    scalars_ref, row_ref, spec_ref, old_ref, old_other_ref, keep_ref, send_ref, weight_ref,
    inv_one_ref, inv_two_ref, now_ref, total_ref, cross_ref,
):
    count = spec_ref.shape[0]
    fill_inverse(row_ref, inv_one_ref, inv_two_ref)
    total_ref[...] = jnp.zeros_like(total_ref)
    weight_ref[...] = jnp.zeros_like(weight_ref)
    real, imag, last_re, last_im, scale = unpack(scalars_ref[CORE], old_ref, old_other_ref)
    is_first = iota((ROWS - HALF, K), 0) == 0
    now_ref[:HALF, :] = real * scale
    now_ref[HALF:ROWS, :] = jnp.where(is_first, last_re * scale, 0.0)
    now_ref[ROWS : ROWS + HALF, :] = imag * scale
    now_ref[ROWS + HALF :, :] = jnp.where(is_first, last_im * scale, 0.0)

    def finish(first):
        add_aligned(first, GROUP, scalars_ref, spec_ref, weight_ref, row_ref, total_ref)

    def body(number, _):
        first = number * GROUP
        finish(jnp.maximum(first - GROUP, 0))
        correlate(first, GROUP, spec_ref, now_ref, cross_ref, inv_one_ref, inv_two_ref, weight_ref)
        return 0

    lax.fori_loop(0, count // GROUP, body, 0)
    finish(count - GROUP)
    pack(scalars_ref[CORE], total_ref, keep_ref, send_ref)


def last_kernel(scalars_ref, old_ref, old_other_ref, out_ref):
    real, imag, last_re, last_im, scale = unpack(scalars_ref[CORE], old_ref, old_other_ref)
    turn = one_at(HALF - iota((HALF, HALF), 0), iota((HALF, HALF), 1))
    back = one_at(column_order(iota((K, K), 0)) & (K - 1), iota((K, K), 1))
    is_first = iota((HALF, K), 0) == 0
    for part, (body, row_128) in enumerate(((real, last_re), (imag, last_im))):
        turned = negate_columns(dot(turn, body.astype(BF16)))
        turned = jnp.where(is_first, row_128, turned if part == 0 else -turned)
        both = jnp.concatenate([body, turned], axis=0)
        natural = sum(dot(piece, back) for piece in split(both))
        out_ref[part] = natural * scale


def params(mebibytes):
    return pltpu.CompilerParams(vmem_limit_bytes=mebibytes * 1024 * 1024)


SCALARS = pl.BlockSpec(memory_space=pltpu.SMEM)
VMEM = pl.BlockSpec(memory_space=pltpu.VMEM)
HBM = pl.BlockSpec(memory_space=pltpu.HBM)
HALF_SHAPE = (SLICES, 2 * DEEP, 128)
TABLES = [((K, K), BF16), ((2 * ROWS, K), BF16), ((2 * K, 2 * K), BF16), ((K, K), BF16)]
WORK = [((2 * ROWS, K), F32), ((2 * ROWS, K), F32), ((GROUP * ROWS, 2 * K), BF16)]


def scratch(*shapes):
    return [pltpu.VMEM(*shape) for shape in shapes]


def in_hbm(array):
    return pltpu.with_memory_space_constraint(array, pltpu.HBM)


def run_first(patterns, ref_spectrum, scalars, bins):
    count = patterns.shape[0]
    return pl.pallas_call(
        first_kernel,
        out_shape=(
            pltpu.VMEM((count, 2 * ROWS, K), BF16),
            pltpu.VMEM(HALF_SHAPE, F32),
            pltpu.VMEM(HALF_SHAPE, BF16),
            pltpu.VMEM((bins, K, K), BF16),
        ),
        in_specs=[SCALARS, VMEM, HBM, HBM],
        out_specs=(VMEM, VMEM, VMEM, VMEM),
        scratch_shapes=scratch(
            (patterns.shape, BF16), (ref_spectrum.shape, F32), *TABLES, *WORK, ((count, 128), F32)
        )
        + [pltpu.SemaphoreType.DMA, pltpu.SemaphoreType.DMA((count // GROUP,))],
        compiler_params=params(32),
        cost_estimate=pl.CostEstimate(flops=int(4e9), bytes_accessed=int(12e6), transcendentals=0),
        name="forward_and_correlate",
    )(scalars, jnp.asarray(cosine_row()), in_hbm(patterns), in_hbm(ref_spectrum))


def run_second(spectra, keep, other, scalars):
    count = spectra.shape[0]
    return pl.pallas_call(
        second_kernel,
        out_shape=(
            pltpu.VMEM(HALF_SHAPE, F32),
            pltpu.VMEM(HALF_SHAPE, BF16),
            pltpu.VMEM((count, 128), F32),
        ),
        in_specs=[SCALARS, VMEM, VMEM, VMEM, VMEM],
        out_specs=(VMEM, VMEM, VMEM),
        scratch_shapes=scratch(*TABLES[2:], *WORK),
        compiler_params=params(32),
        cost_estimate=pl.CostEstimate(flops=int(3e9), bytes_accessed=int(4e6), transcendentals=0),
        name="correlate_again",
    )(scalars, jnp.asarray(cosine_row()), spectra, keep, other)


def run_last(keep, other, scalars):
    return pl.pallas_call(
        last_kernel,
        out_shape=jax.ShapeDtypeStruct((2, K, K), F32),
        in_specs=[SCALARS, VMEM, VMEM],
        out_specs=VMEM,
        compiler_params=params(16),
        cost_estimate=pl.CostEstimate(flops=int(1e8), bytes_accessed=int(1e6), transcendentals=0),
        name="finish",
    )(scalars, keep, other)


def add_halves(*halves):
    values = [half.astype(F32) for half in halves]
    while len(values) > 1:
        values = [values[i] + values[i + 1] for i in range(0, len(values), 2)]
    return values[0].astype(BF16)


def on_device(patterns, ref_spectrum, shifts, bin_owner, bin_index):
    columns, lines = lax.axis_size("col"), lax.axis_size("row")
    me = lax.axis_index("col")
    owner = bin_owner.reshape(-1)
    chips = columns // 2
    targets = ((owner ^ me) % 2) * (chips * BINS) + ((owner // 2) ^ (me // 2)) * BINS + bin_index
    scalars = jnp.concatenate([shifts.reshape(-1), targets, (me % 2).reshape(1).astype(jnp.int32)])

    def send(array, far, axis="col"):
        return lax.ppermute(array, axis, [(i, i ^ far) for i in range(lax.axis_size(axis))])

    def over_chips(half):
        return [half] + [send(half, 2 * far) for far in range(1, chips)]

    def over_lines(half):
        return [half] + [send(half, far, "row") for far in range(1, lines)]

    spectra, keep, away, bins = run_first(patterns, ref_spectrum, scalars, columns * BINS)
    mine, other, other_far = jnp.split(bins, (chips * BINS, (2 * chips - 1) * BINS))
    half = add_halves(keep, send(away, 1))
    half, other, other_far = lax.optimization_barrier((half, other, other_far))
    half = add_halves(*over_chips(half))
    other, other_far = send(other, 1), send(other_far, 1)
    mine = mine.reshape(chips, BINS, K, K)
    other = other.reshape(chips - 1, BINS, K, K)

    def chip_bins(far, *more, low=0, high=BINS):
        there = other[far] if far < chips - 1 else other_far
        arrays = [array[low:high].astype(F32) for array in (mine[far], there, *more)]
        return sum(arrays[1:], arrays[0])

    binned = chip_bins(0)
    if chips == 4:
        block = chip_bins(3).astype(BF16)
        half, block = lax.optimization_barrier((half, block))
        pairs = lambda hops: [(2 * a + core, 2 * b + core) for a, b in hops for core in range(2)]
        passing = lax.ppermute(block, "col", pairs([(0, 1), (3, 2)]))
        middle = lax.ppermute(block, "col", pairs([(1, 2), (2, 1)]))
        half = add_halves(*over_lines(half))
        other_half = send(half, 1)
        half, passing, middle = lax.optimization_barrier((half, passing, middle))
        cut = BINS // 2
        blocks = [
            (chip_bins(1, low=low, high=high).astype(BF16), chip_bins(2, passing, low=low, high=high).astype(BF16))
            for low, high in ((0, cut), (cut, BINS))
        ]
        half, other_half, blocks = lax.optimization_barrier((half, other_half, blocks))
        lower = (send(blocks[0][0], 2), send(blocks[0][1], 4))
        keep, away, weight = run_second(spectra, half, other_half, scalars)
        away, lower = lax.optimization_barrier((away, lower))
        upper = (send(blocks[1][0], 2), send(blocks[1][1], 4))
        halves = over_lines(add_halves(keep, send(away, 1)))
        halves, upper = lax.optimization_barrier((halves, upper))
        half = add_halves(*halves)
        binned = binned + middle.astype(F32)
        for a, b in zip(lower, upper):
            binned = binned + jnp.concatenate([a, b]).astype(F32)
    else:
        half = add_halves(*over_lines(half))
        for far in range(1, chips):
            binned = binned + send(chip_bins(far).astype(BF16), 2 * far).astype(F32)
        keep, away, weight = run_second(spectra, half, send(half, 1), scalars)
        half = add_halves(*over_lines(add_halves(keep, send(away, 1))))
    half = add_halves(*over_chips(half))
    return (run_last(half, send(half, 1), scalars), weight[:, 0], binned)


def solution(mesh):
    placed = (P(BOTH, None, None), P(), P(BOTH, None), P(BOTH, None), P(BOTH))
    return jax.shard_map(
        on_device,
        mesh=mesh,
        in_specs=placed,
        out_specs=(P(), P(BOTH), P(BOTH, None, None)),
        check_vma=False,
    )
```

```python
import functools
import math

import jax
import jax.numpy as jnp
import ml_dtypes
import numpy as np
from jax import lax
from jax.experimental import pallas as pl
from jax.experimental.pallas import tpu as pltpu
from jax.sharding import PartitionSpec as P

BINS = 4
ITERS = 2
K = 256
HALF = K // 2
ROWS = HALF + 16
REACH = 16
DEEP = 8
SLICES = HALF // DEEP
BOTH = ("row", "col")
F32 = jnp.float32
BF16 = jnp.bfloat16


@functools.cache
def cosine_row():
    angle = np.arange(HALF).astype(np.float32) * np.float32(2.0 * math.pi / K)
    return np.broadcast_to(np.cos(angle).astype(np.float32), (8, HALF))


def iota(shape, axis):
    return lax.broadcasted_iota(jnp.int32, shape, axis)


def cosine(row_ref, turns):
    rows, lanes = turns.shape
    row = jnp.broadcast_to(row_ref[:1, :], (rows, HALF))
    found = []
    for first in range(0, lanes, HALF):
        part = turns[:, first : first + HALF]
        value = jnp.take_along_axis(row, part & (HALF - 1), axis=1, mode="promise_in_bounds")
        found.append(jnp.where((part & HALF) == 0, value, -value))
    return found[0] if len(found) == 1 else jnp.concatenate(found, axis=1)


QUARTER = K // 4


def column_order(index):
    return jnp.where(index <= HALF, index, HALF - index)


def fill_forward(row_ref, fwd_one_ref, fwd_two_ref):
    lane = iota((K, K), 1)
    turns = iota((K, K), 0) * jnp.where(lane <= HALF, lane, lane - HALF)
    fwd_one_ref[...] = cosine(row_ref, turns - jnp.where(lane <= HALF, 0, QUARTER)).astype(BF16)
    row = iota((ROWS, K), 0)
    turns = row * iota((ROWS, K), 1)
    for part in range(2):
        table = jnp.where(row <= HALF, cosine(row_ref, turns + part * QUARTER), 0.0)
        fwd_two_ref[part * ROWS : (part + 1) * ROWS, :] = table.astype(BF16)


def fill_inverse(row_ref, inv_one_ref, inv_two_ref):
    row, lane = iota((K, K), 0), iota((K, K), 1)
    turns = column_order(row) * lane
    even, odd = cosine(row_ref, turns).astype(BF16), cosine(row_ref, turns - QUARTER).astype(BF16)
    inv_one_ref[:K, :K] = even
    inv_one_ref[:K, K:] = odd
    inv_one_ref[K:, :K] = -odd
    inv_one_ref[K:, K:] = even
    turns = row * jnp.where(lane <= HALF, lane, lane - HALF) + jnp.where(lane <= HALF, 0, QUARTER)
    scale = jnp.where((lane == 0) | (lane == HALF), 1.0, 2.0)
    inv_two_ref[...] = (scale * cosine(row_ref, turns).astype(BF16).astype(F32)).astype(BF16)


def one_at(rows, lanes):
    return jnp.where(rows == lanes, 1.0, 0.0).astype(BF16)


def dot(a, b):
    return jnp.dot(a, b, preferred_element_type=F32)


def split(a):
    high = a.astype(BF16)
    return (high, (a - high.astype(F32)).astype(BF16))


def negate_columns(a):
    turned = jnp.concatenate([a[:, HALF:], a[:, :HALF]], axis=1)
    lane = lax.broadcasted_iota(jnp.int32, a.shape, 1)
    return jnp.where((lane == 0) | (lane == HALF), a, turned)


def hermitian_part(ref_ref, now_ref):
    reorder = one_at(iota((K, K), 0), column_order(iota((K, K), 1)) & (K - 1))
    row = iota((ROWS, K), 0)
    turn = one_at(jnp.where(row <= HALF, (K - row) & (K - 1), -1), iota((ROWS, K), 1))
    for part, sign in ((0, 1.0), (1, -1.0)):
        straight = jnp.zeros((ROWS, K), F32)
        turned = jnp.zeros((ROWS, K), F32)
        for piece in split(ref_ref[part]):
            piece = dot(piece, reorder).astype(BF16)
            straight = straight + piece[:ROWS].astype(F32)
            turned = turned + dot(turn, piece)
        now_ref[part * ROWS : (part + 1) * ROWS, :] = 0.5 * (straight + sign * negate_columns(turned))


def unpack(core, keep_ref, other_ref):
    halves = []
    for ref in (keep_ref, other_ref):
        rows = []
        for number in range(SLICES):
            piece = ref[number].astype(F32)
            rows.append(jnp.concatenate([piece[:DEEP], piece[DEEP:]], axis=1))
        halves.append(jnp.concatenate(rows, axis=0))
    keep, other = halves
    real, imag = jnp.where(core == 0, keep, other), jnp.where(core == 0, other, keep)
    zero_re, zero_im = real[:1], imag[:1]
    turn_re, turn_im = negate_columns(real[:8])[:1], negate_columns(imag[:8])[:1]
    power = (
        2.0 * jnp.sum(real * real + imag * imag, axis=(0, 1), keepdims=True)
        - jnp.sum(zero_re * zero_re + zero_im * zero_im, axis=(0, 1), keepdims=True)
    ) * (1.0 / (K * K))
    is_first = lax.broadcasted_iota(jnp.int32, (HALF, K), 0) == 0
    real = jnp.where(is_first, 0.5 * (zero_re + turn_re), real)
    imag = jnp.where(is_first, 0.5 * (zero_im - turn_im), imag)
    last_re = 0.5 * (zero_im + turn_im)
    last_im = 0.5 * (turn_re - zero_re)
    return (real, imag, last_re, last_im, lax.rsqrt(power + 1e-06))


def pack(core, total_ref, keep_ref, send_ref):
    is_first = lax.broadcasted_iota(jnp.int32, (HALF, K), 0) == 0
    real = total_ref[:HALF, :]
    imag = total_ref[ROWS : ROWS + HALF, :]
    last_re = total_ref[HALF : HALF + 1, :]
    last_im = total_ref[ROWS + HALF : ROWS + HALF + 1, :]
    real, imag = jnp.where(is_first, real - last_im, real), jnp.where(is_first, imag + last_re, imag)
    for ref, half in ((keep_ref, jnp.where(core == 0, real, imag)), (send_ref, jnp.where(core == 0, imag, real))):
        for number in range(SLICES):
            piece = half[number * DEEP : (number + 1) * DEEP]
            ref[number] = jnp.concatenate([piece[:, :128], piece[:, 128:]], axis=0).astype(ref.dtype)


def forward(first, size, pattern_ref, spec_ref, fwd_one_ref, fwd_two_ref):
    flat = pattern_ref[pl.ds(first, size)].reshape(size * K, K)
    half = dot(flat, fwd_one_ref[...]).astype(BF16)
    is_zero = lax.broadcasted_iota(jnp.int32, (ROWS, HALF), 1) == 0
    for number in range(size):
        both = dot(fwd_two_ref[...], half[number * K : (number + 1) * K])
        cu, cv = both[:ROWS, :HALF], both[:ROWS, HALF:]
        su, sv = both[ROWS:, :HALF], both[ROWS:, HALF:]
        real = jnp.concatenate([cu + jnp.where(is_zero, 0.0, sv), jnp.where(is_zero, cv, cu - sv)], axis=1)
        imag = jnp.concatenate([su - jnp.where(is_zero, 0.0, cv), jnp.where(is_zero, sv, su + cv)], axis=1)
        spec_ref[first + number] = jnp.concatenate([real, imag], axis=0).astype(BF16)


def correlate(first, size, spec_ref, now_ref, cross_ref, inv_one_ref, inv_two_ref, weight_ref):
    for number in range(size):
        spec_re = spec_ref[first + number, :ROWS, :].astype(F32)
        spec_im = spec_ref[first + number, ROWS:, :].astype(F32)
        now_re, now_im = now_ref[:ROWS, :], now_ref[ROWS:, :]
        rows = slice(number * ROWS, (number + 1) * ROWS)
        cross_ref[rows, :K] = (spec_re * now_re + spec_im * now_im).astype(BF16)
        cross_ref[rows, K:] = (spec_im * now_re - spec_re * now_im).astype(BF16)
    both = dot(cross_ref[...], inv_one_ref[...])
    is_first = lax.broadcasted_iota(jnp.int32, (HALF, K), 0) == 0
    for number in range(size):
        mid = both[number * ROWS : (number + 1) * ROWS]
        lower = jnp.where(is_first, mid[HALF : HALF + 1, :K], mid[:HALF, K:])
        corr = dot(inv_two_ref[...], jnp.concatenate([mid[:HALF, :K], lower], axis=0).astype(BF16))
        peak = jnp.max(corr, axis=(0, 1), keepdims=True) * (1.0 / (K * K))
        mean = jnp.sum(corr * corr, axis=(0, 1), keepdims=True) * (1.0 / float(K) ** 6)
        weight = peak / jnp.sqrt(mean + 1e-06)
        weight_ref[pl.ds(first + number, 1), :] = jnp.broadcast_to(weight, (1, 128))


def add_aligned(first, size, scalars_ref, spec_ref, weight_ref, row_ref, total_ref):
    total_re, total_im = total_ref[:ROWS, :], total_ref[ROWS:, :]
    lane = iota((8, K), 1)
    for number in range(size):
        shift_y, shift_x = scalars_ref[2 * (first + number)], scalars_ref[2 * (first + number) + 1]
        weight = weight_ref[pl.ds(first + number, 1), :]
        weight = jnp.concatenate([weight, weight], axis=1)
        turns = column_order(lane) * shift_x
        across_re = weight * cosine(row_ref, turns)[:1]
        across_im = weight * cosine(row_ref, turns + QUARTER)[:1]
        turns = iota((ROWS, HALF), 0) * shift_y
        down_re, down_im = cosine(row_ref, turns), cosine(row_ref, turns + QUARTER)
        down_re = jnp.concatenate([down_re, down_re], axis=1)
        down_im = jnp.concatenate([down_im, down_im], axis=1)
        ramp_re = down_re * across_re - down_im * across_im
        ramp_im = down_re * across_im + down_im * across_re
        spec_re = spec_ref[first + number, :ROWS, :].astype(F32)
        spec_im = spec_ref[first + number, ROWS:, :].astype(F32)
        total_re = total_re + (spec_re * ramp_re - spec_im * ramp_im)
        total_im = total_im + (spec_im * ramp_re + spec_re * ramp_im)
    total_ref[:ROWS, :] = total_re
    total_ref[ROWS:, :] = total_im


def add_bins(first, size, scalars_ref, pattern_ref, weight_ref, bins_ref):
    for number in range(size):
        weight = weight_ref[pl.ds(first + number, 1), :]
        weight = jnp.concatenate([weight, weight], axis=1)
        scaled = (weight * pattern_ref[first + number].astype(F32)).astype(BF16)
        slot = scalars_ref[TARGET + first + number]
        bins_ref[slot] = bins_ref[slot] + scaled


GROUP = 4
COUNT = 16
TARGET = 2 * COUNT
CORE = 3 * COUNT


def first_kernel(
    scalars_ref, row_ref, pattern_hbm, ref_hbm, spec_ref, keep_ref, send_ref, bins_ref,
    pattern_ref, ref_ref, fwd_one_ref, fwd_two_ref, inv_one_ref, inv_two_ref, now_ref, total_ref, cross_ref,
    weight_ref, ref_sem, pattern_sem,
):
    count = pattern_ref.shape[0]
    groups = count // GROUP

    def fetch(number):
        source, target = (ref.at[pl.ds(number * GROUP, GROUP)] for ref in (pattern_hbm, pattern_ref))
        return pltpu.make_async_copy(source, target, pattern_sem.at[number])

    ref_copy = pltpu.make_async_copy(ref_hbm, ref_ref, ref_sem)
    ref_copy.start()
    for number in range(groups):
        fetch(number).start()
    fill_forward(row_ref, fwd_one_ref, fwd_two_ref)
    fill_inverse(row_ref, inv_one_ref, inv_two_ref)
    total_ref[...] = jnp.zeros_like(total_ref)
    bins_ref[...] = jnp.zeros_like(bins_ref)
    weight_ref[...] = jnp.zeros_like(weight_ref)
    spec_ref[:GROUP] = jnp.zeros_like(spec_ref[:GROUP])
    ref_copy.wait()
    hermitian_part(ref_ref, now_ref)

    def finish(first):
        add_aligned(first, GROUP, scalars_ref, spec_ref, weight_ref, row_ref, total_ref)

    def body(number, _):
        first = number * GROUP
        fetch(number).wait()
        finish(jnp.maximum(first - GROUP, 0))
        forward(first, GROUP, pattern_ref, spec_ref, fwd_one_ref, fwd_two_ref)
        correlate(first, GROUP, spec_ref, now_ref, cross_ref, inv_one_ref, inv_two_ref, weight_ref)
        add_bins(first, GROUP, scalars_ref, pattern_ref, weight_ref, bins_ref)
        return 0

    lax.fori_loop(0, groups, body, 0)
    finish(count - GROUP)
    pack(scalars_ref[CORE], total_ref, keep_ref, send_ref)


def second_kernel(
    scalars_ref, row_ref, spec_ref, old_ref, old_other_ref, keep_ref, send_ref, weight_ref,
    inv_one_ref, inv_two_ref, now_ref, total_ref, cross_ref,
):
    count = spec_ref.shape[0]
    fill_inverse(row_ref, inv_one_ref, inv_two_ref)
    total_ref[...] = jnp.zeros_like(total_ref)
    weight_ref[...] = jnp.zeros_like(weight_ref)
    real, imag, last_re, last_im, scale = unpack(scalars_ref[CORE], old_ref, old_other_ref)
    is_first = iota((ROWS - HALF, K), 0) == 0
    now_ref[:HALF, :] = real * scale
    now_ref[HALF:ROWS, :] = jnp.where(is_first, last_re * scale, 0.0)
    now_ref[ROWS : ROWS + HALF, :] = imag * scale
    now_ref[ROWS + HALF :, :] = jnp.where(is_first, last_im * scale, 0.0)

    def finish(first):
        add_aligned(first, GROUP, scalars_ref, spec_ref, weight_ref, row_ref, total_ref)

    def body(number, _):
        first = number * GROUP
        finish(jnp.maximum(first - GROUP, 0))
        correlate(first, GROUP, spec_ref, now_ref, cross_ref, inv_one_ref, inv_two_ref, weight_ref)
        return 0

    lax.fori_loop(0, count // GROUP, body, 0)
    finish(count - GROUP)
    pack(scalars_ref[CORE], total_ref, keep_ref, send_ref)


def last_kernel(scalars_ref, old_ref, old_other_ref, out_ref):
    real, imag, last_re, last_im, scale = unpack(scalars_ref[CORE], old_ref, old_other_ref)
    turn = one_at(HALF - iota((HALF, HALF), 0), iota((HALF, HALF), 1))
    back = one_at(column_order(iota((K, K), 0)) & (K - 1), iota((K, K), 1))
    is_first = iota((HALF, K), 0) == 0
    for part, (body, row_128) in enumerate(((real, last_re), (imag, last_im))):
        turned = negate_columns(dot(turn, body.astype(BF16)))
        turned = jnp.where(is_first, row_128, turned if part == 0 else -turned)
        both = jnp.concatenate([body, turned], axis=0)
        natural = sum(dot(piece, back) for piece in split(both))
        out_ref[part] = natural * scale


def params(mebibytes):
    return pltpu.CompilerParams(vmem_limit_bytes=mebibytes * 1024 * 1024)


SCALARS = pl.BlockSpec(memory_space=pltpu.SMEM)
VMEM = pl.BlockSpec(memory_space=pltpu.VMEM)
HBM = pl.BlockSpec(memory_space=pltpu.HBM)
HALF_SHAPE = (SLICES, 2 * DEEP, 128)
TABLES = [((K, K), BF16), ((2 * ROWS, K), BF16), ((2 * K, 2 * K), BF16), ((K, K), BF16)]
WORK = [((2 * ROWS, K), F32), ((2 * ROWS, K), F32), ((GROUP * ROWS, 2 * K), BF16)]


def scratch(*shapes):
    return [pltpu.VMEM(*shape) for shape in shapes]


def in_hbm(array):
    return pltpu.with_memory_space_constraint(array, pltpu.HBM)


def run_first(patterns, ref_spectrum, scalars, bins):
    count = patterns.shape[0]
    return pl.pallas_call(
        first_kernel,
        out_shape=(
            pltpu.VMEM((count, 2 * ROWS, K), BF16),
            pltpu.VMEM(HALF_SHAPE, F32),
            pltpu.VMEM(HALF_SHAPE, BF16),
            pltpu.VMEM((bins, K, K), BF16),
        ),
        in_specs=[SCALARS, VMEM, HBM, HBM],
        out_specs=(VMEM, VMEM, VMEM, VMEM),
        scratch_shapes=scratch(
            (patterns.shape, BF16), (ref_spectrum.shape, F32), *TABLES, *WORK, ((count, 128), F32)
        )
        + [pltpu.SemaphoreType.DMA, pltpu.SemaphoreType.DMA((count // GROUP,))],
        compiler_params=params(32),
        cost_estimate=pl.CostEstimate(flops=int(4e9), bytes_accessed=int(12e6), transcendentals=0),
        name="forward_and_correlate",
    )(scalars, jnp.asarray(cosine_row()), in_hbm(patterns), in_hbm(ref_spectrum))


def run_second(spectra, keep, other, scalars):
    count = spectra.shape[0]
    return pl.pallas_call(
        second_kernel,
        out_shape=(
            pltpu.VMEM(HALF_SHAPE, F32),
            pltpu.VMEM(HALF_SHAPE, BF16),
            pltpu.VMEM((count, 128), F32),
        ),
        in_specs=[SCALARS, VMEM, VMEM, VMEM, VMEM],
        out_specs=(VMEM, VMEM, VMEM),
        scratch_shapes=scratch(*TABLES[2:], *WORK),
        compiler_params=params(32),
        cost_estimate=pl.CostEstimate(flops=int(3e9), bytes_accessed=int(4e6), transcendentals=0),
        name="correlate_again",
    )(scalars, jnp.asarray(cosine_row()), spectra, keep, other)


def run_last(keep, other, scalars):
    return pl.pallas_call(
        last_kernel,
        out_shape=jax.ShapeDtypeStruct((2, K, K), F32),
        in_specs=[SCALARS, VMEM, VMEM],
        out_specs=VMEM,
        compiler_params=params(16),
        cost_estimate=pl.CostEstimate(flops=int(1e8), bytes_accessed=int(1e6), transcendentals=0),
        name="finish",
    )(scalars, keep, other)


def add_halves(*halves):
    values = [half.astype(F32) for half in halves]
    while len(values) > 1:
        values = [values[i] + values[i + 1] for i in range(0, len(values), 2)]
    return values[0].astype(BF16)


def on_device(patterns, ref_spectrum, shifts, bin_owner, bin_index):
    columns, lines = lax.axis_size("col"), lax.axis_size("row")
    me = lax.axis_index("col")
    owner = bin_owner.reshape(-1)
    chips = columns // 2
    targets = ((owner ^ me) % 2) * (chips * BINS) + ((owner // 2) ^ (me // 2)) * BINS + bin_index
    scalars = jnp.concatenate([shifts.reshape(-1), targets, (me % 2).reshape(1).astype(jnp.int32)])

    def send(array, far, axis="col"):
        return lax.ppermute(array, axis, [(i, i ^ far) for i in range(lax.axis_size(axis))])

    def over_chips(half):
        return [half] + [send(half, 2 * far) for far in range(1, chips)]

    def over_lines(half):
        return [half] + [send(half, far, "row") for far in range(1, lines)]

    spectra, keep, away, bins = run_first(patterns, ref_spectrum, scalars, columns * BINS)
    mine, other, other_far = jnp.split(bins, (chips * BINS, (2 * chips - 1) * BINS))
    half = add_halves(keep, send(away, 1))
    half, other, other_far = lax.optimization_barrier((half, other, other_far))
    half = add_halves(*over_chips(half))
    other, other_far = send(other, 1), send(other_far, 1)
    mine = mine.reshape(chips, BINS, K, K)
    other = other.reshape(chips - 1, BINS, K, K)

    def chip_bins(far, *more):
        there = other[far] if far < chips - 1 else other_far
        arrays = [array.astype(F32) for array in (mine[far], there, *more)]
        return sum(arrays[1:], arrays[0])

    binned = chip_bins(0)
    if chips == 4:
        block = chip_bins(3).astype(BF16)
        half, block = lax.optimization_barrier((half, block))
        pairs = lambda hops: [(2 * a + core, 2 * b + core) for a, b in hops for core in range(2)]
        passing = lax.ppermute(block, "col", pairs([(0, 1), (3, 2)]))
        middle = lax.ppermute(block, "col", pairs([(1, 2), (2, 1)]))
        half = add_halves(*over_lines(half))
        other_half = send(half, 1)
        arrived = [middle, send(chip_bins(1).astype(BF16), 2), send(chip_bins(2, passing).astype(BF16), 4)]
        keep, away, weight = run_second(spectra, half, send(half, 1), scalars)
        halves = over_lines(add_halves(keep, send(away, 1)))
        halves, arrived = lax.optimization_barrier((halves, arrived))
        half = add_halves(*halves)
        binned = sum([array.astype(F32) for array in arrived], binned)
    else:
        half = add_halves(*over_lines(half))
        for far in range(1, chips):
            binned = binned + send(chip_bins(far).astype(BF16), 2 * far).astype(F32)
        keep, away, weight = run_second(spectra, half, send(half, 1), scalars)
        half = add_halves(*over_lines(add_halves(keep, send(away, 1))))
    half = add_halves(*over_chips(half))
    return (run_last(half, send(half, 1), scalars), weight[:, 0], binned)


def solution(mesh):
    placed = (P(BOTH, None, None), P(), P(BOTH, None), P(BOTH, None), P(BOTH))
    return jax.shard_map(
        on_device,
        mesh=mesh,
        in_specs=placed,
        out_specs=(P(), P(BOTH), P(BOTH, None, None)),
        check_vma=False,
    )
```

```python
import functools
import math

import jax
import jax.numpy as jnp
import ml_dtypes
import numpy as np
from jax import lax
from jax.experimental import pallas as pl
from jax.experimental.pallas import tpu as pltpu
from jax.sharding import PartitionSpec as P

BINS = 4
ITERS = 2
K = 256
HALF = K // 2
ROWS = HALF + 16
REACH = 16
DEEP = 8
SLICES = HALF // DEEP
BOTH = ("row", "col")
F32 = jnp.float32
BF16 = jnp.bfloat16


@functools.cache
def cosine_row():
    angle = np.arange(HALF).astype(np.float32) * np.float32(2.0 * math.pi / K)
    return np.broadcast_to(np.cos(angle).astype(np.float32), (8, HALF))


def iota(shape, axis):
    return lax.broadcasted_iota(jnp.int32, shape, axis)


def cosine(row_ref, turns):
    rows, lanes = turns.shape
    row = jnp.broadcast_to(row_ref[:1, :], (rows, HALF))
    found = []
    for first in range(0, lanes, HALF):
        part = turns[:, first : first + HALF]
        value = jnp.take_along_axis(row, part & (HALF - 1), axis=1, mode="promise_in_bounds")
        found.append(jnp.where((part & HALF) == 0, value, -value))
    return found[0] if len(found) == 1 else jnp.concatenate(found, axis=1)


QUARTER = K // 4


def column_order(index):
    return jnp.where(index <= HALF, index, HALF - index)


def fill_forward(row_ref, fwd_one_ref, fwd_two_ref):
    lane = iota((K, K), 1)
    turns = iota((K, K), 0) * jnp.where(lane <= HALF, lane, lane - HALF)
    fwd_one_ref[...] = cosine(row_ref, turns - jnp.where(lane <= HALF, 0, QUARTER)).astype(BF16)
    row = iota((ROWS, K), 0)
    turns = row * iota((ROWS, K), 1)
    for part in range(2):
        table = jnp.where(row <= HALF, cosine(row_ref, turns + part * QUARTER), 0.0)
        fwd_two_ref[part * ROWS : (part + 1) * ROWS, :] = table.astype(BF16)


def fill_inverse(row_ref, inv_one_ref, inv_two_ref):
    row, lane = iota((K, K), 0), iota((K, K), 1)
    turns = column_order(row) * lane
    even, odd = cosine(row_ref, turns).astype(BF16), cosine(row_ref, turns - QUARTER).astype(BF16)
    inv_one_ref[:K, :K] = even
    inv_one_ref[:K, K:] = odd
    inv_one_ref[K:, :K] = -odd
    inv_one_ref[K:, K:] = even
    turns = row * jnp.where(lane <= HALF, lane, lane - HALF) + jnp.where(lane <= HALF, 0, QUARTER)
    scale = jnp.where((lane == 0) | (lane == HALF), 1.0, 2.0)
    inv_two_ref[...] = (scale * cosine(row_ref, turns).astype(BF16).astype(F32)).astype(BF16)


def one_at(rows, lanes):
    return jnp.where(rows == lanes, 1.0, 0.0).astype(BF16)


def dot(a, b):
    return jnp.dot(a, b, preferred_element_type=F32)


def split(a):
    high = a.astype(BF16)
    return (high, (a - high.astype(F32)).astype(BF16))


def negate_columns(a):
    turned = jnp.concatenate([a[:, HALF:], a[:, :HALF]], axis=1)
    lane = lax.broadcasted_iota(jnp.int32, a.shape, 1)
    return jnp.where((lane == 0) | (lane == HALF), a, turned)


def hermitian_part(ref_ref, now_ref):
    reorder = one_at(iota((K, K), 0), column_order(iota((K, K), 1)) & (K - 1))
    row = iota((ROWS, K), 0)
    turn = one_at(jnp.where(row <= HALF, (K - row) & (K - 1), -1), iota((ROWS, K), 1))
    for part, sign in ((0, 1.0), (1, -1.0)):
        straight = jnp.zeros((ROWS, K), F32)
        turned = jnp.zeros((ROWS, K), F32)
        for piece in split(ref_ref[part]):
            piece = dot(piece, reorder).astype(BF16)
            straight = straight + piece[:ROWS].astype(F32)
            turned = turned + dot(turn, piece)
        now_ref[part * ROWS : (part + 1) * ROWS, :] = 0.5 * (straight + sign * negate_columns(turned))


def unpack(core, keep_ref, other_ref):
    halves = []
    for ref in (keep_ref, other_ref):
        rows = []
        for number in range(SLICES):
            piece = ref[number].astype(F32)
            rows.append(jnp.concatenate([piece[:DEEP], piece[DEEP:]], axis=1))
        halves.append(jnp.concatenate(rows, axis=0))
    keep, other = halves
    real, imag = jnp.where(core == 0, keep, other), jnp.where(core == 0, other, keep)
    zero_re, zero_im = real[:1], imag[:1]
    turn_re, turn_im = negate_columns(real[:8])[:1], negate_columns(imag[:8])[:1]
    power = (
        2.0 * jnp.sum(real * real + imag * imag, axis=(0, 1), keepdims=True)
        - jnp.sum(zero_re * zero_re + zero_im * zero_im, axis=(0, 1), keepdims=True)
    ) * (1.0 / (K * K))
    is_first = lax.broadcasted_iota(jnp.int32, (HALF, K), 0) == 0
    real = jnp.where(is_first, 0.5 * (zero_re + turn_re), real)
    imag = jnp.where(is_first, 0.5 * (zero_im - turn_im), imag)
    last_re = 0.5 * (zero_im + turn_im)
    last_im = 0.5 * (turn_re - zero_re)
    return (real, imag, last_re, last_im, lax.rsqrt(power + 1e-06))


def pack(core, total_ref, keep_ref, send_ref):
    is_first = lax.broadcasted_iota(jnp.int32, (HALF, K), 0) == 0
    real = total_ref[:HALF, :]
    imag = total_ref[ROWS : ROWS + HALF, :]
    last_re = total_ref[HALF : HALF + 1, :]
    last_im = total_ref[ROWS + HALF : ROWS + HALF + 1, :]
    real, imag = jnp.where(is_first, real - last_im, real), jnp.where(is_first, imag + last_re, imag)
    for ref, half in ((keep_ref, jnp.where(core == 0, real, imag)), (send_ref, jnp.where(core == 0, imag, real))):
        for number in range(SLICES):
            piece = half[number * DEEP : (number + 1) * DEEP]
            ref[number] = jnp.concatenate([piece[:, :128], piece[:, 128:]], axis=0).astype(ref.dtype)


def forward(first, size, pattern_ref, spec_ref, fwd_one_ref, fwd_two_ref):
    flat = pattern_ref[pl.ds(first, size)].reshape(size * K, K)
    half = dot(flat, fwd_one_ref[...]).astype(BF16)
    is_zero = lax.broadcasted_iota(jnp.int32, (ROWS, HALF), 1) == 0
    for number in range(size):
        both = dot(fwd_two_ref[...], half[number * K : (number + 1) * K])
        cu, cv = both[:ROWS, :HALF], both[:ROWS, HALF:]
        su, sv = both[ROWS:, :HALF], both[ROWS:, HALF:]
        real = jnp.concatenate([cu + jnp.where(is_zero, 0.0, sv), jnp.where(is_zero, cv, cu - sv)], axis=1)
        imag = jnp.concatenate([su - jnp.where(is_zero, 0.0, cv), jnp.where(is_zero, sv, su + cv)], axis=1)
        spec_ref[first + number] = jnp.concatenate([real, imag], axis=0).astype(BF16)


def correlate(first, size, spec_ref, now_ref, cross_ref, inv_one_ref, inv_two_ref, weight_ref):
    for number in range(size):
        spec_re = spec_ref[first + number, :ROWS, :].astype(F32)
        spec_im = spec_ref[first + number, ROWS:, :].astype(F32)
        now_re, now_im = now_ref[:ROWS, :], now_ref[ROWS:, :]
        rows = slice(number * ROWS, (number + 1) * ROWS)
        cross_ref[rows, :K] = (spec_re * now_re + spec_im * now_im).astype(BF16)
        cross_ref[rows, K:] = (spec_im * now_re - spec_re * now_im).astype(BF16)
    both = dot(cross_ref[...], inv_one_ref[...])
    is_first = lax.broadcasted_iota(jnp.int32, (HALF, K), 0) == 0
    for number in range(size):
        mid = both[number * ROWS : (number + 1) * ROWS]
        lower = jnp.where(is_first, mid[HALF : HALF + 1, :K], mid[:HALF, K:])
        corr = dot(inv_two_ref[...], jnp.concatenate([mid[:HALF, :K], lower], axis=0).astype(BF16))
        peak = jnp.max(corr, axis=(0, 1), keepdims=True) * (1.0 / (K * K))
        mean = jnp.sum(corr * corr, axis=(0, 1), keepdims=True) * (1.0 / float(K) ** 6)
        weight = peak / jnp.sqrt(mean + 1e-06)
        weight_ref[pl.ds(first + number, 1), :] = jnp.broadcast_to(weight, (1, 128))


def add_aligned(first, size, scalars_ref, spec_ref, weight_ref, row_ref, total_ref):
    total_re, total_im = total_ref[:ROWS, :], total_ref[ROWS:, :]
    lane = iota((8, K), 1)
    for number in range(size):
        shift_y, shift_x = scalars_ref[first + number], scalars_ref[COUNT + first + number]
        weight = weight_ref[pl.ds(first + number, 1), :]
        weight = jnp.concatenate([weight, weight], axis=1)
        turns = column_order(lane) * shift_x
        across_re = weight * cosine(row_ref, turns)[:1]
        across_im = weight * cosine(row_ref, turns + QUARTER)[:1]
        turns = iota((ROWS, HALF), 0) * shift_y
        down_re, down_im = cosine(row_ref, turns), cosine(row_ref, turns + QUARTER)
        down_re = jnp.concatenate([down_re, down_re], axis=1)
        down_im = jnp.concatenate([down_im, down_im], axis=1)
        ramp_re = down_re * across_re - down_im * across_im
        ramp_im = down_re * across_im + down_im * across_re
        spec_re = spec_ref[first + number, :ROWS, :].astype(F32)
        spec_im = spec_ref[first + number, ROWS:, :].astype(F32)
        total_re = total_re + (spec_re * ramp_re - spec_im * ramp_im)
        total_im = total_im + (spec_im * ramp_re + spec_re * ramp_im)
    total_ref[:ROWS, :] = total_re
    total_ref[ROWS:, :] = total_im


def add_bins(first, size, scalars_ref, pattern_ref, weight_ref, bins_ref):
    for number in range(size):
        weight = weight_ref[pl.ds(first + number, 1), :]
        weight = jnp.concatenate([weight, weight], axis=1)
        scaled = (weight * pattern_ref[first + number].astype(F32)).astype(BF16)
        slot = scalars_ref[TARGET + first + number]
        bins_ref[slot] = bins_ref[slot] + scaled


GROUP = 4
COUNT = 16
TARGET = 2 * COUNT
CORE = 3 * COUNT


def first_kernel(
    scalars_ref, row_ref, pattern_hbm, ref_hbm, spec_ref, keep_ref, send_ref, bins_ref,
    pattern_ref, ref_ref, fwd_one_ref, fwd_two_ref, inv_one_ref, inv_two_ref, now_ref, total_ref, cross_ref,
    weight_ref, ref_sem, pattern_sem,
):
    count = pattern_ref.shape[0]
    groups = count // GROUP

    def fetch(number):
        source, target = (ref.at[pl.ds(number * GROUP, GROUP)] for ref in (pattern_hbm, pattern_ref))
        return pltpu.make_async_copy(source, target, pattern_sem.at[number])

    ref_copy = pltpu.make_async_copy(ref_hbm, ref_ref, ref_sem)
    ref_copy.start()
    for number in range(groups):
        fetch(number).start()
    fill_forward(row_ref, fwd_one_ref, fwd_two_ref)
    fill_inverse(row_ref, inv_one_ref, inv_two_ref)
    total_ref[...] = jnp.zeros_like(total_ref)
    bins_ref[...] = jnp.zeros_like(bins_ref)
    weight_ref[...] = jnp.zeros_like(weight_ref)
    spec_ref[:GROUP] = jnp.zeros_like(spec_ref[:GROUP])
    ref_copy.wait()
    hermitian_part(ref_ref, now_ref)

    def finish(first):
        add_aligned(first, GROUP, scalars_ref, spec_ref, weight_ref, row_ref, total_ref)

    def body(number, _):
        first = number * GROUP
        fetch(number).wait()
        finish(jnp.maximum(first - GROUP, 0))
        forward(first, GROUP, pattern_ref, spec_ref, fwd_one_ref, fwd_two_ref)
        correlate(first, GROUP, spec_ref, now_ref, cross_ref, inv_one_ref, inv_two_ref, weight_ref)
        add_bins(first, GROUP, scalars_ref, pattern_ref, weight_ref, bins_ref)
        return 0

    lax.fori_loop(0, groups, body, 0)
    finish(count - GROUP)
    pack(scalars_ref[CORE], total_ref, keep_ref, send_ref)


def second_kernel(
    scalars_ref, row_ref, spec_ref, old_ref, old_other_ref, keep_ref, send_ref, weight_ref,
    inv_one_ref, inv_two_ref, now_ref, total_ref, cross_ref,
):
    count = spec_ref.shape[0]
    fill_inverse(row_ref, inv_one_ref, inv_two_ref)
    total_ref[...] = jnp.zeros_like(total_ref)
    weight_ref[...] = jnp.zeros_like(weight_ref)
    real, imag, last_re, last_im, scale = unpack(scalars_ref[CORE], old_ref, old_other_ref)
    is_first = iota((ROWS - HALF, K), 0) == 0
    now_ref[:HALF, :] = real * scale
    now_ref[HALF:ROWS, :] = jnp.where(is_first, last_re * scale, 0.0)
    now_ref[ROWS : ROWS + HALF, :] = imag * scale
    now_ref[ROWS + HALF :, :] = jnp.where(is_first, last_im * scale, 0.0)

    def finish(first):
        add_aligned(first, GROUP, scalars_ref, spec_ref, weight_ref, row_ref, total_ref)

    def body(number, _):
        first = number * GROUP
        finish(jnp.maximum(first - GROUP, 0))
        correlate(first, GROUP, spec_ref, now_ref, cross_ref, inv_one_ref, inv_two_ref, weight_ref)
        return 0

    lax.fori_loop(0, count // GROUP, body, 0)
    finish(count - GROUP)
    pack(scalars_ref[CORE], total_ref, keep_ref, send_ref)


def last_kernel(scalars_ref, old_ref, old_other_ref, out_ref):
    real, imag, last_re, last_im, scale = unpack(scalars_ref[CORE], old_ref, old_other_ref)
    turn = one_at(HALF - iota((HALF, HALF), 0), iota((HALF, HALF), 1))
    back = one_at(column_order(iota((K, K), 0)) & (K - 1), iota((K, K), 1))
    is_first = iota((HALF, K), 0) == 0
    for part, (body, row_128) in enumerate(((real, last_re), (imag, last_im))):
        turned = negate_columns(dot(turn, body.astype(BF16)))
        turned = jnp.where(is_first, row_128, turned if part == 0 else -turned)
        both = jnp.concatenate([body, turned], axis=0)
        natural = sum(dot(piece, back) for piece in split(both))
        out_ref[part] = natural * scale


def params(mebibytes):
    return pltpu.CompilerParams(vmem_limit_bytes=mebibytes * 1024 * 1024)


SCALARS = pl.BlockSpec(memory_space=pltpu.SMEM)
VMEM = pl.BlockSpec(memory_space=pltpu.VMEM)
HBM = pl.BlockSpec(memory_space=pltpu.HBM)
HALF_SHAPE = (SLICES, 2 * DEEP, 128)
TABLES = [((K, K), BF16), ((2 * ROWS, K), BF16), ((2 * K, 2 * K), BF16), ((K, K), BF16)]
WORK = [((2 * ROWS, K), F32), ((2 * ROWS, K), F32), ((GROUP * ROWS, 2 * K), BF16)]


def scratch(*shapes):
    return [pltpu.VMEM(*shape) for shape in shapes]


def in_hbm(array):
    return pltpu.with_memory_space_constraint(array, pltpu.HBM)


def run_first(patterns, ref_spectrum, scalars, bins):
    count = patterns.shape[0]
    return pl.pallas_call(
        first_kernel,
        out_shape=(
            pltpu.VMEM((count, 2 * ROWS, K), BF16),
            pltpu.VMEM(HALF_SHAPE, F32),
            pltpu.VMEM(HALF_SHAPE, BF16),
            pltpu.VMEM((bins, K, K), BF16),
        ),
        in_specs=[SCALARS, VMEM, HBM, HBM],
        out_specs=(VMEM, VMEM, VMEM, VMEM),
        scratch_shapes=scratch(
            (patterns.shape, BF16), (ref_spectrum.shape, F32), *TABLES, *WORK, ((count, 128), F32)
        )
        + [pltpu.SemaphoreType.DMA, pltpu.SemaphoreType.DMA((count // GROUP,))],
        compiler_params=params(32),
        cost_estimate=pl.CostEstimate(flops=int(4e9), bytes_accessed=int(12e6), transcendentals=0),
        name="forward_and_correlate",
    )(scalars, jnp.asarray(cosine_row()), in_hbm(patterns), in_hbm(ref_spectrum))


def run_second(spectra, keep, other, scalars):
    count = spectra.shape[0]
    return pl.pallas_call(
        second_kernel,
        out_shape=(
            pltpu.VMEM(HALF_SHAPE, F32),
            pltpu.VMEM(HALF_SHAPE, BF16),
            pltpu.VMEM((count, 128), F32),
        ),
        in_specs=[SCALARS, VMEM, VMEM, VMEM, VMEM],
        out_specs=(VMEM, VMEM, VMEM),
        scratch_shapes=scratch(*TABLES[2:], *WORK),
        compiler_params=params(32),
        cost_estimate=pl.CostEstimate(flops=int(3e9), bytes_accessed=int(4e6), transcendentals=0),
        name="correlate_again",
    )(scalars, jnp.asarray(cosine_row()), spectra, keep, other)


def run_last(keep, other, scalars):
    return pl.pallas_call(
        last_kernel,
        out_shape=jax.ShapeDtypeStruct((2, K, K), F32),
        in_specs=[SCALARS, VMEM, VMEM],
        out_specs=VMEM,
        compiler_params=params(16),
        cost_estimate=pl.CostEstimate(flops=int(1e8), bytes_accessed=int(1e6), transcendentals=0),
        name="finish",
    )(scalars, keep, other)


def add_halves(*halves):
    values = [half.astype(F32) for half in halves]
    while len(values) > 1:
        values = [values[i] + values[i + 1] for i in range(0, len(values), 2)]
    return values[0].astype(BF16)


def on_device(patterns, ref_spectrum, shifts, bin_owner, bin_index):
    columns, lines = lax.axis_size("col"), lax.axis_size("row")
    me = lax.axis_index("col")
    owner = bin_owner.reshape(-1)
    chips = columns // 2
    targets = ((owner ^ me) % 2) * (chips * BINS) + ((owner // 2) ^ (me // 2)) * BINS + bin_index
    scalars = jnp.concatenate([shifts[:, 0], shifts[:, 1], targets, (me % 2).reshape(1).astype(jnp.int32)])

    def send(array, far, axis="col"):
        return lax.ppermute(array, axis, [(i, i ^ far) for i in range(lax.axis_size(axis))])

    def over_chips(half):
        return [half] + [send(half, 2 * far) for far in range(1, chips)]

    def over_lines(half):
        return [half] + [send(half, far, "row") for far in range(1, lines)]

    spectra, keep, away, bins = run_first(patterns, ref_spectrum, scalars, columns * BINS)
    mine, other, other_far = jnp.split(bins, (chips * BINS, (2 * chips - 1) * BINS))
    half = add_halves(keep, send(away, 1))
    half, other, other_far = lax.optimization_barrier((half, other, other_far))
    halves = over_chips(half)
    other, other_far = send(other, 1), send(other_far, 1)
    mine = mine.reshape(chips, BINS, K, K)
    other = other.reshape(chips - 1, BINS, K, K)

    def chip_bins(far, *more):
        there = other[far] if far < chips - 1 else other_far
        arrays = [array.astype(F32) for array in (mine[far], there, *more)]
        return sum(arrays[1:], arrays[0])

    binned = chip_bins(0)
    if chips == 4:
        block = chip_bins(3).astype(BF16)
        second, first = chip_bins(2).astype(BF16), chip_bins(1).astype(BF16)
        halves[3], block, second, first = lax.optimization_barrier((halves[3], block, second, first))
        half = add_halves(*halves)
        pairs = lambda hops: [(2 * a + core, 2 * b + core) for a, b in hops for core in range(2)]
        passing = lax.ppermute(block, "col", pairs([(0, 1), (3, 2)]))
        middle = lax.ppermute(block, "col", pairs([(1, 2), (2, 1)]))
        ends = lax.ppermute(second, "col", pairs([(0, 2), (3, 1)]))
        half = add_halves(*over_lines(half))
        near = send(first, 2)
        inner = lax.ppermute(chip_bins(2, passing).astype(BF16), "col", pairs([(1, 3), (2, 0)]))
        keep, away, weight = run_second(spectra, half, send(half, 1), scalars)
        away, middle, ends = lax.optimization_barrier((away, middle, ends))
        halves = over_lines(add_halves(keep, send(away, 1)))
        halves, near, inner = lax.optimization_barrier((halves, near, inner))
        half = add_halves(*halves)
        binned = sum([array.astype(F32) for array in (middle, ends, near, inner)], binned)
    else:
        half = add_halves(*over_lines(add_halves(*halves)))
        for far in range(1, chips):
            binned = binned + send(chip_bins(far).astype(BF16), 2 * far).astype(F32)
        keep, away, weight = run_second(spectra, half, send(half, 1), scalars)
        half = add_halves(*over_lines(add_halves(keep, send(away, 1))))
    half = add_halves(*over_chips(half))
    return (run_last(half, send(half, 1), scalars), weight[:, 0], binned)


def solution(mesh):
    placed = (P(BOTH, None, None), P(), P(BOTH, None), P(BOTH, None), P(BOTH))
    return jax.shard_map(
        on_device,
        mesh=mesh,
        in_specs=placed,
        out_specs=(P(), P(BOTH), P(BOTH, None, None)),
        check_vma=False,
    )
```

```python
import math

import jax
import jax.numpy as jnp
from jax import lax
from jax.experimental import pallas as pl
from jax.experimental.pallas import tpu as pltpu
from jax.sharding import PartitionSpec as P

BINS = 4
ITERS = 2
K = 256
HALF = K // 2
ROWS = HALF + 16
REACH = 16
DEEP = 8
SLICES = HALF // DEEP
BOTH = ("row", "col")
F32 = jnp.float32
BF16 = jnp.bfloat16


def iota(shape, axis):
    return lax.broadcasted_iota(jnp.int32, shape, axis)


def cosine(row_ref, turns):
    rows, lanes = turns.shape
    row = jnp.broadcast_to(row_ref[:1, :], (rows, HALF))
    found = []
    for first in range(0, lanes, HALF):
        part = turns[:, first : first + HALF]
        value = jnp.take_along_axis(row, part & (HALF - 1), axis=1, mode="promise_in_bounds")
        found.append(jnp.where((part & HALF) == 0, value, -value))
    return found[0] if len(found) == 1 else jnp.concatenate(found, axis=1)


QUARTER = K // 4


def column_order(index):
    return jnp.where(index <= HALF, index, HALF - index)


def quarter_tables(row_ref):
    row, lane = iota((HALF, HALF), 0), iota((HALF, HALF), 1)
    turns = row * lane
    by_row, by_lane = (jnp.where((index & 1) == 0, 1.0, -1.0) for index in (row, lane))
    return cosine(row_ref, turns), cosine(row_ref, turns - QUARTER), by_row, by_lane, lane == 0


def beside(a, b):
    return jnp.concatenate([a, b], axis=1)


def fill_forward(row_ref, fwd_one_ref, fwd_two_ref):
    even, odd, by_row, by_lane, at_zero = quarter_tables(row_ref)
    fwd_one_ref[:HALF, :] = beside(even, jnp.where(at_zero, by_row, odd)).astype(BF16)
    fwd_one_ref[HALF:, :] = beside(even * by_lane, jnp.where(at_zero, by_row, odd * by_lane)).astype(BF16)
    pad = iota((ROWS - HALF, K), 0)
    last = jnp.where((iota((ROWS - HALF, K), 1) & 1) == 0, 1.0, -1.0)
    fwd_two_ref[:HALF, :] = beside(even, even * by_row).astype(BF16)
    fwd_two_ref[HALF:ROWS, :] = jnp.where(pad == 0, last, 0.0).astype(BF16)
    fwd_two_ref[ROWS : ROWS + HALF, :] = beside(-odd, -odd * by_row).astype(BF16)
    fwd_two_ref[ROWS + HALF :, :] = jnp.zeros((ROWS - HALF, K), BF16)


def fill_inverse(row_ref, inv_one_ref, inv_two_ref):
    even, odd, by_row, by_lane, at_zero = quarter_tables(row_ref)
    real, imag = beside(even, even * by_row), beside(odd, odd * by_row)
    is_first = iota((HALF, K), 0) == 0
    parity = jnp.where((iota((HALF, K), 1) & 1) == 0, 1.0, -1.0)
    real_back, imag_back = jnp.where(is_first, parity, real), jnp.where(is_first, 0.0, -imag)
    for first, re, im in ((0, real, imag), (HALF, real_back, imag_back)):
        inv_one_ref[first : first + HALF, :K] = re.astype(BF16)
        inv_one_ref[first : first + HALF, K:] = im.astype(BF16)
        inv_one_ref[K + first : K + first + HALF, :K] = (-im).astype(BF16)
        inv_one_ref[K + first : K + first + HALF, K:] = re.astype(BF16)
    for first, sign in ((0, 1.0), (HALF, by_lane)):
        left = jnp.where(at_zero, 1.0, 2.0 * sign * even)
        right = jnp.where(at_zero, by_row, -2.0 * sign * odd)
        inv_two_ref[first : first + HALF, :] = beside(left, right).astype(BF16)


def one_at(rows, lanes):
    return jnp.where(rows == lanes, 1.0, 0.0).astype(BF16)


def dot(a, b):
    return jnp.dot(a, b, preferred_element_type=F32)


def split(a):
    high = a.astype(BF16)
    return (high, (a - high.astype(F32)).astype(BF16))


def negate_columns(a):
    turned = jnp.concatenate([a[:, HALF:], a[:, :HALF]], axis=1)
    lane = lax.broadcasted_iota(jnp.int32, a.shape, 1)
    return jnp.where((lane == 0) | (lane == HALF), a, turned)


def hermitian_part(ref_ref, now_ref):
    reorder = one_at(iota((K, K), 0), column_order(iota((K, K), 1)) & (K - 1))
    row = iota((ROWS, K), 0)
    turn = one_at(jnp.where(row <= HALF, (K - row) & (K - 1), -1), iota((ROWS, K), 1))
    for part, sign in ((0, 1.0), (1, -1.0)):
        straight = jnp.zeros((ROWS, K), F32)
        turned = jnp.zeros((ROWS, K), F32)
        for piece in split(ref_ref[part]):
            piece = dot(piece, reorder).astype(BF16)
            straight = straight + piece[:ROWS].astype(F32)
            turned = turned + dot(turn, piece)
        now_ref[part * ROWS : (part + 1) * ROWS, :] = 0.5 * (straight + sign * negate_columns(turned))


def unpack(core, keep_ref, other_ref):
    halves = []
    for ref in (keep_ref, other_ref):
        rows = []
        for number in range(SLICES):
            piece = ref[number].astype(F32)
            rows.append(jnp.concatenate([piece[:DEEP], piece[DEEP:]], axis=1))
        halves.append(jnp.concatenate(rows, axis=0))
    keep, other = halves
    real, imag = jnp.where(core == 0, keep, other), jnp.where(core == 0, other, keep)
    zero_re, zero_im = real[:1], imag[:1]
    turn_re, turn_im = negate_columns(real[:8])[:1], negate_columns(imag[:8])[:1]
    power = (
        2.0 * jnp.sum(real * real + imag * imag, axis=(0, 1), keepdims=True)
        - jnp.sum(zero_re * zero_re + zero_im * zero_im, axis=(0, 1), keepdims=True)
    ) * (1.0 / (K * K))
    is_first = lax.broadcasted_iota(jnp.int32, (HALF, K), 0) == 0
    real = jnp.where(is_first, 0.5 * (zero_re + turn_re), real)
    imag = jnp.where(is_first, 0.5 * (zero_im - turn_im), imag)
    last_re = 0.5 * (zero_im + turn_im)
    last_im = 0.5 * (turn_re - zero_re)
    return (real, imag, last_re, last_im, lax.rsqrt(power + 1e-06))


def pack(core, total_ref, keep_ref, send_ref):
    is_first = lax.broadcasted_iota(jnp.int32, (HALF, K), 0) == 0
    real = total_ref[:HALF, :]
    imag = total_ref[ROWS : ROWS + HALF, :]
    last_re = total_ref[HALF : HALF + 1, :]
    last_im = total_ref[ROWS + HALF : ROWS + HALF + 1, :]
    real, imag = jnp.where(is_first, real - last_im, real), jnp.where(is_first, imag + last_re, imag)
    for ref, half in ((keep_ref, jnp.where(core == 0, real, imag)), (send_ref, jnp.where(core == 0, imag, real))):
        for number in range(SLICES):
            piece = half[number * DEEP : (number + 1) * DEEP]
            ref[number] = jnp.concatenate([piece[:, :128], piece[:, 128:]], axis=0).astype(ref.dtype)


def forward(first, size, pattern_ref, spec_ref, fwd_one_ref, fwd_two_ref):
    flat = pattern_ref[pl.ds(first, size)].reshape(size * K, K)
    half = dot(flat, fwd_one_ref[...]).astype(BF16)
    is_zero = lax.broadcasted_iota(jnp.int32, (ROWS, HALF), 1) == 0
    for number in range(size):
        both = dot(fwd_two_ref[...], half[number * K : (number + 1) * K])
        cu, cv = both[:ROWS, :HALF], both[:ROWS, HALF:]
        su, sv = both[ROWS:, :HALF], both[ROWS:, HALF:]
        real = jnp.concatenate([cu + jnp.where(is_zero, 0.0, sv), jnp.where(is_zero, cv, cu - sv)], axis=1)
        imag = jnp.concatenate([su - jnp.where(is_zero, 0.0, cv), jnp.where(is_zero, sv, su + cv)], axis=1)
        spec_ref[first + number] = jnp.concatenate([real, imag], axis=0).astype(BF16)


def correlate(first, size, spec_ref, now_ref, cross_ref, inv_one_ref, inv_two_ref, weight_ref):
    for number in range(size):
        spec_re = spec_ref[first + number, :ROWS, :].astype(F32)
        spec_im = spec_ref[first + number, ROWS:, :].astype(F32)
        now_re, now_im = now_ref[:ROWS, :], now_ref[ROWS:, :]
        rows = slice(number * ROWS, (number + 1) * ROWS)
        cross_ref[rows, :K] = (spec_re * now_re + spec_im * now_im).astype(BF16)
        cross_ref[rows, K:] = (spec_im * now_re - spec_re * now_im).astype(BF16)
    both = dot(cross_ref[...], inv_one_ref[...])
    is_first = lax.broadcasted_iota(jnp.int32, (HALF, K), 0) == 0
    for number in range(size):
        mid = both[number * ROWS : (number + 1) * ROWS]
        lower = jnp.where(is_first, mid[HALF : HALF + 1, :K], mid[:HALF, K:])
        corr = dot(inv_two_ref[...], jnp.concatenate([mid[:HALF, :K], lower], axis=0).astype(BF16))
        peak = jnp.max(corr, axis=(0, 1), keepdims=True) * (1.0 / (K * K))
        mean = jnp.sum(corr * corr, axis=(0, 1), keepdims=True) * (1.0 / float(K) ** 6)
        weight = peak / jnp.sqrt(mean + 1e-06)
        weight_ref[pl.ds(first + number, 1), :] = jnp.broadcast_to(weight, (1, 128))


def add_aligned(first, size, scalars_ref, spec_ref, weight_ref, row_ref, total_ref):
    total_re, total_im = total_ref[:ROWS, :], total_ref[ROWS:, :]
    lane = iota((8, K), 1)
    for number in range(size):
        shift_y, shift_x = scalars_ref[first + number], scalars_ref[COUNT + first + number]
        weight = weight_ref[pl.ds(first + number, 1), :]
        weight = jnp.concatenate([weight, weight], axis=1)
        turns = column_order(lane) * shift_x
        across_re = weight * cosine(row_ref, turns)[:1]
        across_im = weight * cosine(row_ref, turns + QUARTER)[:1]
        turns = iota((ROWS, HALF), 0) * shift_y
        down_re, down_im = cosine(row_ref, turns), cosine(row_ref, turns + QUARTER)
        down_re = jnp.concatenate([down_re, down_re], axis=1)
        down_im = jnp.concatenate([down_im, down_im], axis=1)
        ramp_re = down_re * across_re - down_im * across_im
        ramp_im = down_re * across_im + down_im * across_re
        spec_re = spec_ref[first + number, :ROWS, :].astype(F32)
        spec_im = spec_ref[first + number, ROWS:, :].astype(F32)
        total_re = total_re + (spec_re * ramp_re - spec_im * ramp_im)
        total_im = total_im + (spec_im * ramp_re + spec_re * ramp_im)
    total_ref[:ROWS, :] = total_re
    total_ref[ROWS:, :] = total_im


def add_bins(first, size, scalars_ref, pattern_ref, weight_ref, bins_ref):
    for number in range(size):
        weight = weight_ref[pl.ds(first + number, 1), :]
        weight = jnp.concatenate([weight, weight], axis=1)
        scaled = (weight * pattern_ref[first + number].astype(F32)).astype(BF16)
        slot = scalars_ref[TARGET + first + number]
        bins_ref[slot] = bins_ref[slot] + scaled


GROUP = 4
COUNT = 16
TARGET = 2 * COUNT
CORE = 3 * COUNT


def first_kernel(
    scalars_ref, pattern_hbm, ref_hbm, spec_ref, keep_ref, send_ref, bins_ref, row_ref,
    pattern_ref, ref_ref, fwd_one_ref, fwd_two_ref, inv_one_ref, inv_two_ref, now_ref, total_ref, cross_ref,
    weight_ref, ref_sem, pattern_sem,
):
    count = pattern_ref.shape[0]
    groups = count // GROUP

    def fetch(number):
        source, target = (ref.at[pl.ds(number * GROUP, GROUP)] for ref in (pattern_hbm, pattern_ref))
        return pltpu.make_async_copy(source, target, pattern_sem.at[number])

    ref_copy = pltpu.make_async_copy(ref_hbm, ref_ref, ref_sem)
    ref_copy.start()
    for number in range(groups):
        fetch(number).start()
    total_ref[...] = jnp.zeros_like(total_ref)
    bins_ref[...] = jnp.zeros_like(bins_ref)
    weight_ref[...] = jnp.zeros_like(weight_ref)
    spec_ref[:GROUP] = jnp.zeros_like(spec_ref[:GROUP])
    row_ref[...] = jnp.cos(iota((8, HALF), 1).astype(F32) * (2.0 * math.pi / K))
    fill_forward(row_ref, fwd_one_ref, fwd_two_ref)
    fill_inverse(row_ref, inv_one_ref, inv_two_ref)
    ref_copy.wait()
    hermitian_part(ref_ref, now_ref)

    def finish(first):
        add_aligned(first, GROUP, scalars_ref, spec_ref, weight_ref, row_ref, total_ref)

    def body(number, _):
        first = number * GROUP
        fetch(number).wait()
        finish(jnp.maximum(first - GROUP, 0))
        forward(first, GROUP, pattern_ref, spec_ref, fwd_one_ref, fwd_two_ref)
        correlate(first, GROUP, spec_ref, now_ref, cross_ref, inv_one_ref, inv_two_ref, weight_ref)
        add_bins(first, GROUP, scalars_ref, pattern_ref, weight_ref, bins_ref)
        return 0

    lax.fori_loop(0, groups, body, 0)
    finish(count - GROUP)
    pack(scalars_ref[CORE], total_ref, keep_ref, send_ref)


def second_kernel(
    scalars_ref, row_ref, spec_ref, old_ref, old_other_ref, keep_ref, send_ref, weight_ref,
    inv_one_ref, inv_two_ref, now_ref, total_ref, cross_ref,
):
    count = spec_ref.shape[0]
    fill_inverse(row_ref, inv_one_ref, inv_two_ref)
    total_ref[...] = jnp.zeros_like(total_ref)
    weight_ref[...] = jnp.zeros_like(weight_ref)
    real, imag, last_re, last_im, scale = unpack(scalars_ref[CORE], old_ref, old_other_ref)
    is_first = iota((ROWS - HALF, K), 0) == 0
    now_ref[:HALF, :] = real * scale
    now_ref[HALF:ROWS, :] = jnp.where(is_first, last_re * scale, 0.0)
    now_ref[ROWS : ROWS + HALF, :] = imag * scale
    now_ref[ROWS + HALF :, :] = jnp.where(is_first, last_im * scale, 0.0)

    def finish(first):
        add_aligned(first, GROUP, scalars_ref, spec_ref, weight_ref, row_ref, total_ref)

    def body(number, _):
        first = number * GROUP
        finish(jnp.maximum(first - GROUP, 0))
        correlate(first, GROUP, spec_ref, now_ref, cross_ref, inv_one_ref, inv_two_ref, weight_ref)
        return 0

    lax.fori_loop(0, count // GROUP, body, 0)
    finish(count - GROUP)
    pack(scalars_ref[CORE], total_ref, keep_ref, send_ref)


def last_kernel(scalars_ref, old_ref, old_other_ref, out_ref):
    real, imag, last_re, last_im, scale = unpack(scalars_ref[CORE], old_ref, old_other_ref)
    turn = one_at(HALF - iota((HALF, HALF), 0), iota((HALF, HALF), 1))
    back = one_at(column_order(iota((K, K), 0)) & (K - 1), iota((K, K), 1))
    is_first = iota((HALF, K), 0) == 0
    for part, (body, row_128) in enumerate(((real, last_re), (imag, last_im))):
        turned = negate_columns(dot(turn, body.astype(BF16)))
        turned = jnp.where(is_first, row_128, turned if part == 0 else -turned)
        both = jnp.concatenate([body, turned], axis=0)
        natural = sum(dot(piece, back) for piece in split(both))
        out_ref[part] = natural * scale


def params(mebibytes):
    return pltpu.CompilerParams(vmem_limit_bytes=mebibytes * 1024 * 1024)


SCALARS = pl.BlockSpec(memory_space=pltpu.SMEM)
VMEM = pl.BlockSpec(memory_space=pltpu.VMEM)
HBM = pl.BlockSpec(memory_space=pltpu.HBM)
HALF_SHAPE = (SLICES, 2 * DEEP, 128)
TABLES = [((K, K), BF16), ((2 * ROWS, K), BF16), ((2 * K, 2 * K), BF16), ((K, K), BF16)]
WORK = [((2 * ROWS, K), F32), ((2 * ROWS, K), F32), ((GROUP * ROWS, 2 * K), BF16)]


def scratch(*shapes):
    return [pltpu.VMEM(*shape) for shape in shapes]


def in_hbm(array):
    return pltpu.with_memory_space_constraint(array, pltpu.HBM)


def run_first(patterns, ref_spectrum, scalars, bins):
    count = patterns.shape[0]
    return pl.pallas_call(
        first_kernel,
        out_shape=(
            pltpu.VMEM((count, 2 * ROWS, K), BF16),
            pltpu.VMEM(HALF_SHAPE, F32),
            pltpu.VMEM(HALF_SHAPE, BF16),
            pltpu.VMEM((bins, K, K), BF16),
            pltpu.VMEM((8, HALF), F32),
        ),
        in_specs=[SCALARS, HBM, HBM],
        out_specs=(VMEM, VMEM, VMEM, VMEM, VMEM),
        scratch_shapes=scratch(
            (patterns.shape, BF16), (ref_spectrum.shape, F32), *TABLES, *WORK, ((count, 128), F32)
        )
        + [pltpu.SemaphoreType.DMA, pltpu.SemaphoreType.DMA((count // GROUP,))],
        compiler_params=params(32),
        cost_estimate=pl.CostEstimate(flops=int(4e9), bytes_accessed=int(12e6), transcendentals=0),
        name="forward_and_correlate",
    )(scalars, in_hbm(patterns), in_hbm(ref_spectrum))


def run_second(spectra, keep, other, row, scalars):
    count = spectra.shape[0]
    return pl.pallas_call(
        second_kernel,
        out_shape=(
            pltpu.VMEM(HALF_SHAPE, F32),
            pltpu.VMEM(HALF_SHAPE, BF16),
            pltpu.VMEM((count, 128), F32),
        ),
        in_specs=[SCALARS, VMEM, VMEM, VMEM, VMEM],
        out_specs=(VMEM, VMEM, VMEM),
        scratch_shapes=scratch(*TABLES[2:], *WORK),
        compiler_params=params(32),
        cost_estimate=pl.CostEstimate(flops=int(3e9), bytes_accessed=int(4e6), transcendentals=0),
        name="correlate_again",
    )(scalars, row, spectra, keep, other)


def run_last(keep, other, scalars):
    return pl.pallas_call(
        last_kernel,
        out_shape=jax.ShapeDtypeStruct((2, K, K), F32),
        in_specs=[SCALARS, VMEM, VMEM],
        out_specs=VMEM,
        compiler_params=params(16),
        cost_estimate=pl.CostEstimate(flops=int(1e8), bytes_accessed=int(1e6), transcendentals=0),
        name="finish",
    )(scalars, keep, other)


def add_halves(*halves):
    values = [half.astype(F32) for half in halves]
    while len(values) > 1:
        values = [values[i] + values[i + 1] for i in range(0, len(values), 2)]
    return values[0].astype(BF16)


def on_device(patterns, ref_spectrum, shifts, bin_owner, bin_index):
    columns, lines = lax.axis_size("col"), lax.axis_size("row")
    me = lax.axis_index("col")
    owner = bin_owner.reshape(-1)
    chips = columns // 2
    targets = ((owner ^ me) % 2) * (chips * BINS) + ((owner // 2) ^ (me // 2)) * BINS + bin_index
    scalars = jnp.concatenate([shifts[:, 0], shifts[:, 1], targets, (me % 2).reshape(1).astype(jnp.int32)])

    def send(array, far, axis="col"):
        return lax.ppermute(array, axis, [(i, i ^ far) for i in range(lax.axis_size(axis))])

    def over_chips(half):
        return [half] + [send(half, 2 * far) for far in range(1, chips)]

    def over_lines(half):
        return [half] + [send(half, far, "row") for far in range(1, lines)]

    spectra, keep, away, bins, row = run_first(patterns, ref_spectrum, scalars, columns * BINS)
    mine, other, other_far = jnp.split(bins, (chips * BINS, (2 * chips - 1) * BINS))
    half = add_halves(keep, send(away, 1))
    half, other, other_far = lax.optimization_barrier((half, other, other_far))
    halves = over_chips(half)
    other, other_far = send(other, 1), send(other_far, 1)
    mine = mine.reshape(chips, BINS, K, K)
    other = other.reshape(chips - 1, BINS, K, K)

    def chip_bins(far, *more):
        there = other[far] if far < chips - 1 else other_far
        arrays = [array.astype(F32) for array in (mine[far], there, *more)]
        return sum(arrays[1:], arrays[0])

    binned = chip_bins(0)
    if chips == 4:
        block = chip_bins(3).astype(BF16)
        second, first = chip_bins(2).astype(BF16), chip_bins(1).astype(BF16)
        halves[3], block, second, first = lax.optimization_barrier((halves[3], block, second, first))
        half = add_halves(*halves)
        pairs = lambda hops: [(2 * a + core, 2 * b + core) for a, b in hops for core in range(2)]
        passing = lax.ppermute(block, "col", pairs([(0, 1), (3, 2)]))
        middle = lax.ppermute(block, "col", pairs([(1, 2), (2, 1)]))
        ends = lax.ppermute(second, "col", pairs([(0, 2), (3, 1)]))
        half = add_halves(*over_lines(half))
        near = send(first, 2)
        inner = lax.ppermute(chip_bins(2, passing).astype(BF16), "col", pairs([(1, 3), (2, 0)]))
        keep, away, weight = run_second(spectra, half, send(half, 1), row, scalars)
        away, middle, ends = lax.optimization_barrier((away, middle, ends))
        halves = over_lines(add_halves(keep, send(away, 1)))
        halves, near, inner = lax.optimization_barrier((halves, near, inner))
        half = add_halves(*halves)
        binned = sum([array.astype(F32) for array in (middle, ends, near, inner)], binned)
    else:
        half = add_halves(*over_lines(add_halves(*halves)))
        for far in range(1, chips):
            binned = binned + send(chip_bins(far).astype(BF16), 2 * far).astype(F32)
        keep, away, weight = run_second(spectra, half, send(half, 1), row, scalars)
        half = add_halves(*over_lines(add_halves(keep, send(away, 1))))
    half = add_halves(*over_chips(half))
    return (run_last(half, send(half, 1), scalars), weight[:, 0], binned)


def solution(mesh):
    placed = (P(BOTH, None, None), P(), P(BOTH, None), P(BOTH, None), P(BOTH))
    return jax.shard_map(
        on_device,
        mesh=mesh,
        in_specs=placed,
        out_specs=(P(), P(BOTH), P(BOTH, None, None)),
        check_vma=False,
    )
```

```python
import math

import jax
import jax.numpy as jnp
from jax import lax
from jax.experimental import pallas as pl
from jax.experimental.pallas import tpu as pltpu
from jax.sharding import PartitionSpec as P

BINS = 4
K = 256
HALF = K // 2
ROWS = HALF + 16
REACH = 16
DEEP = 8
SLICES = HALF // DEEP
BOTH = ("row", "col")
F32 = jnp.float32
BF16 = jnp.bfloat16


def iota(shape, axis):
    return lax.broadcasted_iota(jnp.int32, shape, axis)


def cosine(row_ref, turns):
    rows, lanes = turns.shape
    row = jnp.broadcast_to(row_ref[:1, :], (rows, HALF))
    found = []
    for first in range(0, lanes, HALF):
        part = turns[:, first : first + HALF]
        value = jnp.take_along_axis(row, part & (HALF - 1), axis=1, mode="promise_in_bounds")
        found.append(jnp.where((part & HALF) == 0, value, -value))
    return found[0] if len(found) == 1 else jnp.concatenate(found, axis=1)


QUARTER = K // 4


def column_order(index):
    return jnp.where(index <= HALF, index, HALF - index)


def quarter_tables(row_ref):
    row, lane = iota((HALF, HALF), 0), iota((HALF, HALF), 1)
    turns = row * lane
    by_row, by_lane = (jnp.where((index & 1) == 0, 1.0, -1.0) for index in (row, lane))
    return cosine(row_ref, turns), cosine(row_ref, turns - QUARTER), by_row, by_lane, lane == 0


def beside(a, b):
    return jnp.concatenate([a, b], axis=1)


def fill_forward(row_ref, fwd_one_ref, fwd_two_ref):
    even, odd, by_row, by_lane, at_zero = quarter_tables(row_ref)
    fwd_one_ref[:HALF, :] = beside(even, jnp.where(at_zero, by_row, odd)).astype(BF16)
    fwd_one_ref[HALF:, :] = beside(even * by_lane, jnp.where(at_zero, by_row, odd * by_lane)).astype(BF16)
    pad = iota((ROWS - HALF, K), 0)
    last = jnp.where((iota((ROWS - HALF, K), 1) & 1) == 0, 1.0, -1.0)
    fwd_two_ref[:HALF, :] = beside(even, even * by_row).astype(BF16)
    fwd_two_ref[HALF:ROWS, :] = jnp.where(pad == 0, last, 0.0).astype(BF16)
    fwd_two_ref[ROWS : ROWS + HALF, :] = beside(-odd, -odd * by_row).astype(BF16)
    fwd_two_ref[ROWS + HALF :, :] = jnp.zeros((ROWS - HALF, K), BF16)


def fill_inverse(row_ref, inv_one_ref, inv_two_ref):
    even, odd, by_row, by_lane, at_zero = quarter_tables(row_ref)
    real, imag = beside(even, even * by_row), beside(odd, odd * by_row)
    is_first = iota((HALF, K), 0) == 0
    parity = jnp.where((iota((HALF, K), 1) & 1) == 0, 1.0, -1.0)
    real_back, imag_back = jnp.where(is_first, parity, real), jnp.where(is_first, 0.0, -imag)
    for first, re, im in ((0, real, imag), (HALF, real_back, imag_back)):
        inv_one_ref[first : first + HALF, :K] = re.astype(BF16)
        inv_one_ref[first : first + HALF, K:] = im.astype(BF16)
        inv_one_ref[K + first : K + first + HALF, :K] = (-im).astype(BF16)
        inv_one_ref[K + first : K + first + HALF, K:] = re.astype(BF16)
    for first, sign in ((0, 1.0), (HALF, by_lane)):
        left = jnp.where(at_zero, 1.0, 2.0 * sign * even)
        right = jnp.where(at_zero, by_row, -2.0 * sign * odd)
        inv_two_ref[first : first + HALF, :] = beside(left, right).astype(BF16)


def one_at(rows, lanes):
    return jnp.where(rows == lanes, 1.0, 0.0).astype(BF16)


def dot(a, b):
    return jnp.dot(a, b, preferred_element_type=F32)


def split(a):
    high = a.astype(BF16)
    return (high, (a - high.astype(F32)).astype(BF16))


def negate_columns(a):
    turned = jnp.concatenate([a[:, HALF:], a[:, :HALF]], axis=1)
    lane = lax.broadcasted_iota(jnp.int32, a.shape, 1)
    return jnp.where((lane == 0) | (lane == HALF), a, turned)


def hermitian_part(ref_ref, now_ref):
    reorder = one_at(iota((K, K), 0), column_order(iota((K, K), 1)) & (K - 1))
    row = iota((ROWS, K), 0)
    turn = one_at(jnp.where(row <= HALF, (K - row) & (K - 1), -1), iota((ROWS, K), 1))
    for part, sign in ((0, 1.0), (1, -1.0)):
        straight = jnp.zeros((ROWS, K), F32)
        turned = jnp.zeros((ROWS, K), F32)
        for piece in split(ref_ref[part]):
            piece = dot(piece, reorder).astype(BF16)
            straight = straight + piece[:ROWS].astype(F32)
            turned = turned + dot(turn, piece)
        now_ref[part * ROWS : (part + 1) * ROWS, :] = 0.5 * (straight + sign * negate_columns(turned))


def unpack(core, keep_ref, other_ref):
    halves = []
    for ref in (keep_ref, other_ref):
        rows = []
        for number in range(SLICES):
            piece = ref[number].astype(F32)
            rows.append(jnp.concatenate([piece[:DEEP], piece[DEEP:]], axis=1))
        halves.append(jnp.concatenate(rows, axis=0))
    keep, other = halves
    real, imag = jnp.where(core == 0, keep, other), jnp.where(core == 0, other, keep)
    zero_re, zero_im = real[:1], imag[:1]
    turn_re, turn_im = negate_columns(real[:8])[:1], negate_columns(imag[:8])[:1]
    power = (
        2.0 * jnp.sum(real * real + imag * imag, axis=(0, 1), keepdims=True)
        - jnp.sum(zero_re * zero_re + zero_im * zero_im, axis=(0, 1), keepdims=True)
    ) * (1.0 / (K * K))
    is_first = lax.broadcasted_iota(jnp.int32, (HALF, K), 0) == 0
    real = jnp.where(is_first, 0.5 * (zero_re + turn_re), real)
    imag = jnp.where(is_first, 0.5 * (zero_im - turn_im), imag)
    last_re = 0.5 * (zero_im + turn_im)
    last_im = 0.5 * (turn_re - zero_re)
    return (real, imag, last_re, last_im, lax.rsqrt(power + 1e-06))


def pack(core, total_ref, keep_ref, send_ref):
    is_first = lax.broadcasted_iota(jnp.int32, (HALF, K), 0) == 0
    real = total_ref[:HALF, :]
    imag = total_ref[ROWS : ROWS + HALF, :]
    last_re = total_ref[HALF : HALF + 1, :]
    last_im = total_ref[ROWS + HALF : ROWS + HALF + 1, :]
    real, imag = jnp.where(is_first, real - last_im, real), jnp.where(is_first, imag + last_re, imag)
    for ref, half in ((keep_ref, jnp.where(core == 0, real, imag)), (send_ref, jnp.where(core == 0, imag, real))):
        for number in range(SLICES):
            piece = half[number * DEEP : (number + 1) * DEEP]
            ref[number] = jnp.concatenate([piece[:, :128], piece[:, 128:]], axis=0).astype(ref.dtype)


def forward(first, size, pattern_ref, spec_ref, fwd_one_ref, fwd_two_ref):
    flat = pattern_ref[pl.ds(first, size)].reshape(size * K, K)
    half = dot(flat, fwd_one_ref[...]).astype(BF16)
    is_zero = lax.broadcasted_iota(jnp.int32, (ROWS, HALF), 1) == 0
    for number in range(size):
        both = dot(fwd_two_ref[...], half[number * K : (number + 1) * K])
        cu, cv = both[:ROWS, :HALF], both[:ROWS, HALF:]
        su, sv = both[ROWS:, :HALF], both[ROWS:, HALF:]
        real = jnp.concatenate([cu + jnp.where(is_zero, 0.0, sv), jnp.where(is_zero, cv, cu - sv)], axis=1)
        imag = jnp.concatenate([su - jnp.where(is_zero, 0.0, cv), jnp.where(is_zero, sv, su + cv)], axis=1)
        spec_ref[first + number] = jnp.concatenate([real, imag], axis=0).astype(BF16)


def correlate(first, size, spec_ref, now_ref, cross_ref, inv_one_ref, inv_two_ref, weight_ref):
    for number in range(size):
        spec_re = spec_ref[first + number, :ROWS, :].astype(F32)
        spec_im = spec_ref[first + number, ROWS:, :].astype(F32)
        now_re, now_im = now_ref[:ROWS, :], now_ref[ROWS:, :]
        rows = slice(number * ROWS, (number + 1) * ROWS)
        cross_ref[rows, :K] = (spec_re * now_re + spec_im * now_im).astype(BF16)
        cross_ref[rows, K:] = (spec_im * now_re - spec_re * now_im).astype(BF16)
    both = dot(cross_ref[...], inv_one_ref[...])
    is_first = lax.broadcasted_iota(jnp.int32, (HALF, K), 0) == 0
    for number in range(size):
        mid = both[number * ROWS : (number + 1) * ROWS]
        lower = jnp.where(is_first, mid[HALF : HALF + 1, :K], mid[:HALF, K:])
        corr = dot(inv_two_ref[...], jnp.concatenate([mid[:HALF, :K], lower], axis=0).astype(BF16))
        peak = jnp.max(corr, axis=(0, 1), keepdims=True) * (1.0 / (K * K))
        mean = jnp.sum(corr * corr, axis=(0, 1), keepdims=True) * (1.0 / float(K) ** 6)
        weight = peak / jnp.sqrt(mean + 1e-06)
        weight_ref[pl.ds(first + number, 1), :] = jnp.broadcast_to(weight, (1, 128))


def add_aligned(first, size, scalars_ref, spec_ref, weight_ref, row_ref, total_ref):
    total_re, total_im = total_ref[:ROWS, :], total_ref[ROWS:, :]
    lane = iota((8, K), 1)
    for number in range(size):
        shift_y, shift_x = scalars_ref[first + number], scalars_ref[COUNT + first + number]
        weight = weight_ref[pl.ds(first + number, 1), :]
        weight = jnp.concatenate([weight, weight], axis=1)
        turns = column_order(lane) * shift_x
        across_re = weight * cosine(row_ref, turns)[:1]
        across_im = weight * cosine(row_ref, turns + QUARTER)[:1]
        turns = iota((ROWS, HALF), 0) * shift_y
        down_re, down_im = cosine(row_ref, turns), cosine(row_ref, turns + QUARTER)
        down_re = jnp.concatenate([down_re, down_re], axis=1)
        down_im = jnp.concatenate([down_im, down_im], axis=1)
        ramp_re = down_re * across_re - down_im * across_im
        ramp_im = down_re * across_im + down_im * across_re
        spec_re = spec_ref[first + number, :ROWS, :].astype(F32)
        spec_im = spec_ref[first + number, ROWS:, :].astype(F32)
        total_re = total_re + (spec_re * ramp_re - spec_im * ramp_im)
        total_im = total_im + (spec_im * ramp_re + spec_re * ramp_im)
    total_ref[:ROWS, :] = total_re
    total_ref[ROWS:, :] = total_im


def add_bins(first, size, scalars_ref, pattern_ref, weight_ref, bins_ref):
    for number in range(size):
        weight = weight_ref[pl.ds(first + number, 1), :]
        weight = jnp.concatenate([weight, weight], axis=1)
        scaled = (weight * pattern_ref[first + number].astype(F32)).astype(BF16)
        slot = scalars_ref[TARGET + first + number]
        bins_ref[slot] = bins_ref[slot] + scaled


GROUP = 4
COUNT = 16
TARGET = 2 * COUNT
CORE = 3 * COUNT


def first_kernel(
    scalars_ref, pattern_hbm, ref_hbm, spec_ref, keep_ref, send_ref, bins_ref, row_ref,
    pattern_ref, ref_ref, fwd_one_ref, fwd_two_ref, inv_one_ref, inv_two_ref, now_ref, total_ref, cross_ref,
    weight_ref, ref_sem, pattern_sem,
):
    count = pattern_ref.shape[0]
    groups = count // GROUP

    def fetch(number):
        source, target = (ref.at[pl.ds(number * GROUP, GROUP)] for ref in (pattern_hbm, pattern_ref))
        return pltpu.make_async_copy(source, target, pattern_sem.at[number])

    ref_copy = pltpu.make_async_copy(ref_hbm, ref_ref, ref_sem)
    ref_copy.start()
    fetch(0).start()
    total_ref[...] = jnp.zeros_like(total_ref)
    bins_ref[...] = jnp.zeros_like(bins_ref)
    weight_ref[...] = jnp.zeros_like(weight_ref)
    spec_ref[:GROUP] = jnp.zeros_like(spec_ref[:GROUP])
    row_ref[...] = jnp.cos(iota((8, HALF), 1).astype(F32) * (2.0 * math.pi / K))
    fill_forward(row_ref, fwd_one_ref, fwd_two_ref)
    fill_inverse(row_ref, inv_one_ref, inv_two_ref)
    ref_copy.wait()
    for number in range(1, groups):
        fetch(number).start()
    hermitian_part(ref_ref, now_ref)

    def finish(first):
        add_aligned(first, GROUP, scalars_ref, spec_ref, weight_ref, row_ref, total_ref)

    def body(number, _):
        first = number * GROUP
        fetch(number).wait()
        finish(jnp.maximum(first - GROUP, 0))
        forward(first, GROUP, pattern_ref, spec_ref, fwd_one_ref, fwd_two_ref)
        correlate(first, GROUP, spec_ref, now_ref, cross_ref, inv_one_ref, inv_two_ref, weight_ref)
        add_bins(first, GROUP, scalars_ref, pattern_ref, weight_ref, bins_ref)
        return 0

    lax.fori_loop(0, groups, body, 0)
    finish(count - GROUP)
    pack(scalars_ref[CORE], total_ref, keep_ref, send_ref)


def second_kernel(
    scalars_ref, row_ref, spec_ref, old_ref, old_other_ref, keep_ref, send_ref, weight_ref,
    inv_one_ref, inv_two_ref, now_ref, total_ref, cross_ref,
):
    count = spec_ref.shape[0]
    fill_inverse(row_ref, inv_one_ref, inv_two_ref)
    total_ref[...] = jnp.zeros_like(total_ref)
    weight_ref[...] = jnp.zeros_like(weight_ref)
    real, imag, last_re, last_im, scale = unpack(scalars_ref[CORE], old_ref, old_other_ref)
    is_first = iota((ROWS - HALF, K), 0) == 0
    now_ref[:HALF, :] = real * scale
    now_ref[HALF:ROWS, :] = jnp.where(is_first, last_re * scale, 0.0)
    now_ref[ROWS : ROWS + HALF, :] = imag * scale
    now_ref[ROWS + HALF :, :] = jnp.where(is_first, last_im * scale, 0.0)

    def finish(first):
        add_aligned(first, GROUP, scalars_ref, spec_ref, weight_ref, row_ref, total_ref)

    def body(number, _):
        first = number * GROUP
        finish(jnp.maximum(first - GROUP, 0))
        correlate(first, GROUP, spec_ref, now_ref, cross_ref, inv_one_ref, inv_two_ref, weight_ref)
        return 0

    lax.fori_loop(0, count // GROUP, body, 0)
    finish(count - GROUP)
    pack(scalars_ref[CORE], total_ref, keep_ref, send_ref)


def last_kernel(scalars_ref, old_ref, old_other_ref, out_ref):
    real, imag, last_re, last_im, scale = unpack(scalars_ref[CORE], old_ref, old_other_ref)
    turn = one_at(HALF - iota((HALF, HALF), 0), iota((HALF, HALF), 1))
    back = one_at(column_order(iota((K, K), 0)) & (K - 1), iota((K, K), 1))
    is_first = iota((HALF, K), 0) == 0
    for part, (body, row_128) in enumerate(((real, last_re), (imag, last_im))):
        turned = negate_columns(dot(turn, body.astype(BF16)))
        turned = jnp.where(is_first, row_128, turned if part == 0 else -turned)
        both = jnp.concatenate([body, turned], axis=0)
        natural = sum(dot(piece, back) for piece in split(both))
        out_ref[part] = natural * scale


def params(mebibytes):
    return pltpu.CompilerParams(vmem_limit_bytes=mebibytes * 1024 * 1024)


SCALARS = pl.BlockSpec(memory_space=pltpu.SMEM)
VMEM = pl.BlockSpec(memory_space=pltpu.VMEM)
HBM = pl.BlockSpec(memory_space=pltpu.HBM)
HALF_SHAPE = (SLICES, 2 * DEEP, 128)
TABLES = [((K, K), BF16), ((2 * ROWS, K), BF16), ((2 * K, 2 * K), BF16), ((K, K), BF16)]
WORK = [((2 * ROWS, K), F32), ((2 * ROWS, K), F32), ((GROUP * ROWS, 2 * K), BF16)]


def scratch(*shapes):
    return [pltpu.VMEM(*shape) for shape in shapes]


def in_hbm(array):
    return pltpu.with_memory_space_constraint(array, pltpu.HBM)


def run_first(patterns, ref_spectrum, scalars, bins):
    count = patterns.shape[0]
    return pl.pallas_call(
        first_kernel,
        out_shape=(
            pltpu.VMEM((count, 2 * ROWS, K), BF16),
            pltpu.VMEM(HALF_SHAPE, F32),
            pltpu.VMEM(HALF_SHAPE, BF16),
            pltpu.VMEM((bins, K, K), BF16),
            pltpu.VMEM((8, HALF), F32),
        ),
        in_specs=[SCALARS, HBM, HBM],
        out_specs=(VMEM, VMEM, VMEM, VMEM, VMEM),
        scratch_shapes=scratch(
            (patterns.shape, BF16), (ref_spectrum.shape, F32), *TABLES, *WORK, ((count, 128), F32)
        )
        + [pltpu.SemaphoreType.DMA, pltpu.SemaphoreType.DMA((count // GROUP,))],
        compiler_params=params(32),
        cost_estimate=pl.CostEstimate(flops=int(4e9), bytes_accessed=int(12e6), transcendentals=0),
        name="forward_and_correlate",
    )(scalars, in_hbm(patterns), in_hbm(ref_spectrum))


def run_second(spectra, keep, other, row, scalars):
    count = spectra.shape[0]
    return pl.pallas_call(
        second_kernel,
        out_shape=(
            pltpu.VMEM(HALF_SHAPE, F32),
            pltpu.VMEM(HALF_SHAPE, BF16),
            pltpu.VMEM((count, 128), F32),
        ),
        in_specs=[SCALARS, VMEM, VMEM, VMEM, VMEM],
        out_specs=(VMEM, VMEM, VMEM),
        scratch_shapes=scratch(*TABLES[2:], *WORK),
        compiler_params=params(32),
        cost_estimate=pl.CostEstimate(flops=int(3e9), bytes_accessed=int(4e6), transcendentals=0),
        name="correlate_again",
    )(scalars, row, spectra, keep, other)


def run_last(keep, other, scalars):
    return pl.pallas_call(
        last_kernel,
        out_shape=jax.ShapeDtypeStruct((2, K, K), F32),
        in_specs=[SCALARS, VMEM, VMEM],
        out_specs=VMEM,
        compiler_params=params(16),
        cost_estimate=pl.CostEstimate(flops=int(1e8), bytes_accessed=int(1e6), transcendentals=0),
        name="finish",
    )(scalars, keep, other)


def add_halves(*halves):
    values = [half.astype(F32) for half in halves]
    while len(values) > 1:
        values = [values[i] + values[i + 1] for i in range(0, len(values), 2)]
    return values[0].astype(BF16)


def on_device(patterns, ref_spectrum, shifts, bin_owner, bin_index):
    columns, lines = lax.axis_size("col"), lax.axis_size("row")
    me = lax.axis_index("col")
    owner = bin_owner.reshape(-1)
    chips = columns // 2
    targets = ((owner ^ me) % 2) * (chips * BINS) + ((owner // 2) ^ (me // 2)) * BINS + bin_index
    scalars = jnp.concatenate([shifts[:, 0], shifts[:, 1], targets, (me % 2).reshape(1).astype(jnp.int32)])

    def send(array, far, axis="col"):
        return lax.ppermute(array, axis, [(i, i ^ far) for i in range(lax.axis_size(axis))])

    def over_chips(half):
        return [half] + [send(half, 2 * far) for far in range(1, chips)]

    def over_lines(half):
        return [half] + [send(half, far, "row") for far in range(1, lines)]

    spectra, keep, away, bins, row = run_first(patterns, ref_spectrum, scalars, columns * BINS)
    mine, other, other_far = jnp.split(bins, (chips * BINS, (2 * chips - 1) * BINS))
    half = add_halves(keep, send(away, 1))
    half, other, other_far = lax.optimization_barrier((half, other, other_far))
    halves = over_chips(half)
    other, other_far = send(other, 1), send(other_far, 1)
    mine = mine.reshape(chips, BINS, K, K)
    other = other.reshape(chips - 1, BINS, K, K)

    def chip_bins(far, *more):
        there = other[far] if far < chips - 1 else other_far
        arrays = [array.astype(F32) for array in (mine[far], there, *more)]
        return sum(arrays[1:], arrays[0])

    binned = chip_bins(0)
    if chips == 4:
        block = chip_bins(3).astype(BF16)
        second, first = chip_bins(2).astype(BF16), chip_bins(1).astype(BF16)
        halves[3], block, second, first = lax.optimization_barrier((halves[3], block, second, first))
        half = add_halves(*halves)
        pairs = lambda hops: [(2 * a + core, 2 * b + core) for a, b in hops for core in range(2)]
        passing = lax.ppermute(block, "col", pairs([(0, 1), (3, 2)]))
        middle = lax.ppermute(block, "col", pairs([(1, 2), (2, 1)]))
        ends = lax.ppermute(second, "col", pairs([(0, 2), (3, 1)]))
        half = add_halves(*over_lines(half))
        near = send(first, 2)
        inner = lax.ppermute(chip_bins(2, passing).astype(BF16), "col", pairs([(1, 3), (2, 0)]))
        keep, away, weight = run_second(spectra, half, send(half, 1), row, scalars)
        away, middle, ends = lax.optimization_barrier((away, middle, ends))
        halves = over_lines(add_halves(keep, send(away, 1)))
        halves, near, inner = lax.optimization_barrier((halves, near, inner))
        half = add_halves(*halves)
        binned = sum([array.astype(F32) for array in (middle, ends, near, inner)], binned)
    else:
        half = add_halves(*over_lines(add_halves(*halves)))
        for far in range(1, chips):
            binned = binned + send(chip_bins(far).astype(BF16), 2 * far).astype(F32)
        keep, away, weight = run_second(spectra, half, send(half, 1), row, scalars)
        half = add_halves(*over_lines(add_halves(keep, send(away, 1))))
    halves, binned = lax.optimization_barrier((over_chips(half), binned))
    half = add_halves(*halves)
    return (run_last(half, send(half, 1), scalars), weight[:, 0], binned)


def solution(mesh):
    placed = (P(BOTH, None, None), P(), P(BOTH, None), P(BOTH, None), P(BOTH))
    return jax.shard_map(
        on_device,
        mesh=mesh,
        in_specs=placed,
        out_specs=(P(), P(BOTH), P(BOTH, None, None)),
        check_vma=False,
    )
```
